32 devices in a mesh: groups: 2 (over x), dom: 16 (over z, y, core).
Axes of the slice: x: 2, y: 2, z: 4, core: 2. Of those that a mesh axis runs over, the one named last changes fastest.
Arguments:
- micrographs: bfloat16 [64, 1024, 1024], P(('groups', 'dom')), parts along dimension 0, may hold values from -6 to 6
- mic_defocus: int32 [64], P(('groups', 'dom')), parts along dimension 0, may hold values from 0 to 15
- defocus: float32 [32], P('groups'), parts along dimension 0, may hold values from 0.5 to 3
- pick_list: int32 [4, 6144], P(None, ('groups', 'dom')), parts along dimension 1, may hold values from -1 to 1535, as said below
- template_bank: bfloat16 [448, 2048], P(('groups', 'dom')), parts along dimension 0, may hold values from -0.125 to 0.125
- rot_index: int32 [100, 36], P('groups'), parts along dimension 0, may hold values from 0 to 223, as said below
Outputs:
- correlation: bfloat16 [3072, 16, 1800], P(('groups', 'dom')), parts along dimension 0
The draws below stay inside these ranges and needn't reach their ends.
There are 2 independent parts, one for each index of `groups`. The reference program is written for one: setup_inputs(seed, part) draws one part's arguments, and reference() takes and returns one part's arrays. A program takes and returns all parts, laid end to end along the dimension named above; each array names one. Nothing has to cross between parts.
Inputs may be any that keep to these rules, and one draw needn't show every extreme that they name: `pick_list`: row 0 is a micrograph of the device that holds the column (its local index), rows 1 and 2 the top-left pixel of a 256 x 256 box inside it, row 3 the particle the box becomes or -1 for an unused column. Every particle is named by exactly one column. The used columns of one device that name particles of one device number 0 or exactly 12; a device has at most 192 used columns, reached on a quarter of the devices. `rot_index`: every bank entry is named at least once.
All inputs are finite; a program needn't handle non-finite values.
Results may differ from the reference program's by a relative error of at most 0.0071.
Values may be sent and summed in bfloat16 or wider, within the bound.
A program may use at most 128 MiB of HBM per device.

```python
import math
import jax
import jax.numpy as jnp
from jax import lax

BOX = 256
K = 32
CLASSES = 50
ROTS = 36
SH = 4
DEFOCI = 16
MIC = 1024
MICS_DEV = 2
P_DEV = 96
TEMPLATES = 1800
SHIFTS = 16
CAP = 12
PICK_CAP = 192
PICKS = 3072
MICS = 32
BANK = 224
N_DOM = 16


def draw_pick_list(key, part):
    group_count = P_DEV // CAP
    half_groups = group_count // 2
    quarter = N_DOM // 4
    remainder = N_DOM - quarter
    total = P_DEV * N_DOM
    key_src, key_slot, key_rows, key_mic, key_top, key_left = jax.random.split(key, 6)
    source_order = jax.random.permutation(key_src, N_DOM)
    heavy_set = source_order[:quarter]
    light_set = source_order[quarter:]
    target_dev = jnp.arange(N_DOM, dtype=jnp.int32)[:, None]
    group_ids = jnp.arange(group_count, dtype=jnp.int32)[None, :]
    heavy_pick = heavy_set[jnp.mod(target_dev + group_ids, quarter)]
    light_pick = light_set[jnp.mod(target_dev + group_ids - half_groups, remainder)]
    group_source = jnp.where(group_ids < half_groups, heavy_pick, light_pick)
    slot_keys = jax.random.split(key_slot, N_DOM)
    slot_perm = jax.vmap(lambda one_key: jax.random.permutation(one_key, P_DEV))(slot_keys)
    slot_source = jnp.take_along_axis(group_source, slot_perm // CAP, axis=1).reshape(-1).astype(jnp.int32)
    order_idx = jnp.argsort(slot_source, stable=True).astype(jnp.int32)
    sorted_source = slot_source[order_idx]
    per_source = jnp.sum((slot_source[None, :] == jnp.arange(N_DOM, dtype=jnp.int32)[:, None]).astype(jnp.int32), axis=1)
    starts = jnp.cumsum(per_source) - per_source
    within = jnp.arange(total, dtype=jnp.int32) - starts[sorted_source]
    row_keys = jax.random.split(key_rows, N_DOM)
    row_perm = jax.vmap(lambda one_key: jax.random.permutation(one_key, PICK_CAP))(row_keys)
    column = sorted_source * PICK_CAP + row_perm[sorted_source, within]
    target_row = jnp.full((PICKS,), -1, jnp.int32).at[column].set(order_idx)
    mic_row = jax.random.randint(key_mic, (PICKS,), 0, MICS_DEV)
    top_row = jax.random.randint(key_top, (PICKS,), 0, MIC - BOX + 1)
    left_row = jax.random.randint(key_left, (PICKS,), 0, MIC - BOX + 1)
    return jnp.stack([mic_row, top_row, left_row, target_row]).astype(jnp.int32)


def draw_rot_index(key, part):
    shuffled = jax.random.permutation(key, TEMPLATES)
    return jnp.mod(shuffled, BANK).reshape(CLASSES, ROTS).astype(jnp.int32)


def place_ends(values, rng, least, high):
    longest = values.shape.index(max(values.shape))
    spots = []
    for shift in (0, 1):
        where = [jax.random.randint(jax.random.fold_in(rng, axis), (), 0, length) for axis, length in enumerate(values.shape)]
        where[longest] = (where[longest] + shift) % values.shape[longest]
        spots.append(tuple(where))
    return values.at[spots[0]].set(least).at[spots[1]].set(high)


def shard_levels(own_key, dims, cuts, smallest, top_value):
    factor_of, own = 1.0, jax.random.fold_in(own_key, 6)
    for position, parts in cuts:
        draws = jnp.exp(jax.random.uniform(jax.random.fold_in(own, position), (parts,), jnp.float32, smallest / len(cuts), top_value / len(cuts)))
        factor_of = factor_of * jnp.repeat(draws, dims[position] // parts).reshape([-1 if axis == position else 1 for axis in range(len(dims))])
    return factor_of


def gaussian(own_key, extent, width, limit, pieces=(), kind=jnp.bfloat16):
    level = shard_levels(own_key, extent, pieces, -0.22, 0.18) if pieces else 1.0
    entries = jax.random.normal(own_key, extent, jnp.float32) * width * level
    return jnp.minimum(jnp.maximum(entries, -limit), limit).astype(kind)


def setup_inputs(seed: int = 0, part: int = 0) -> dict:
    arg_keys = jax.random.split(jax.random.key(seed), 7)
    part_splits = jax.random.split(jax.random.fold_in(arg_keys[6], part), 7)
    micrographs = gaussian(part_splits[0], (MICS, MIC, MIC), 1.0, 6.0, ((0, 16),))
    mic_defocus = place_ends(jax.random.randint(part_splits[1], (MICS,), 0, DEFOCI), jax.random.fold_in(part_splits[1], 1), 0, DEFOCI - 1).astype(jnp.int32)
    defocus = jnp.clip(jnp.exp(jax.random.uniform(part_splits[2], (DEFOCI,), jnp.float32, math.log(0.5), math.log(3.0))), 0.5, 3.0)
    pick_list = draw_pick_list(jax.random.fold_in(jax.random.fold_in(arg_keys[6], part), 71), part)
    template_bank = gaussian(part_splits[4], (BANK, 2 * K * K), (2 * K * K) ** -0.5, 0.125, ((0, 16),))
    rot_index = draw_rot_index(jax.random.fold_in(jax.random.fold_in(arg_keys[6], part), 71), part)
    return {"micrographs": micrographs, "mic_defocus": mic_defocus, "defocus": defocus, "pick_list": pick_list, "template_bank": template_bank, "rot_index": rot_index}


TWO_PI = 2.0 * math.pi
CHI_SCALE = 0.05
CHI_SHIFT = 0.1

def forward_table(box_side, freq_side):
    offsets = jnp.arange(freq_side, dtype=jnp.int32) - freq_side // 2
    pixels = jnp.arange(box_side, dtype=jnp.int32)
    phase_turns = jnp.mod(offsets[:, None] * pixels[None, :], box_side).astype(jnp.float32) / box_side
    norm_scale = 1.0 / math.sqrt(box_side)
    stacked = jnp.concatenate([jnp.cos(TWO_PI * phase_turns) * norm_scale, -jnp.sin(TWO_PI * phase_turns) * norm_scale], axis=0)
    return stacked.astype(jnp.bfloat16)

def ctf_table(defocus, freq_side):
    offsets = (jnp.arange(freq_side, dtype=jnp.int32) - freq_side // 2).astype(jnp.float32)
    radius = (offsets[:, None] * offsets[:, None] + offsets[None, :] * offsets[None, :]).reshape(-1)
    return -jnp.sin(CHI_SCALE * defocus[:, None] * radius[None, :] + CHI_SHIFT)

def shift_tables(box_side, freq_side, shift_side):
    offsets = jnp.arange(freq_side, dtype=jnp.int32) - freq_side // 2
    shift_moves = jnp.arange(shift_side, dtype=jnp.int32) - shift_side // 2
    row_freq = jnp.repeat(offsets, freq_side)
    col_freq = jnp.tile(offsets, freq_side)
    row_move = jnp.repeat(shift_moves, shift_side)
    col_move = jnp.tile(shift_moves, shift_side)
    phase_turns = jnp.mod(row_move[:, None] * row_freq[None, :] + col_move[:, None] * col_freq[None, :], box_side).astype(jnp.float32) / box_side
    return (jnp.cos(TWO_PI * phase_turns), jnp.sin(TWO_PI * phase_turns))

def spectra(box_stack, dft_table, ctf_rows, freq_side):
    first_pass = jnp.einsum('ky,byx->bkx', dft_table.astype(jnp.float32), box_stack.astype(jnp.float32), precision=lax.Precision.HIGHEST).astype(jnp.bfloat16)
    second = jnp.einsum('bkx,jx->bkj', first_pass.astype(jnp.float32), dft_table.astype(jnp.float32), precision=lax.Precision.HIGHEST)
    real_part = second[:, :freq_side, :freq_side] - second[:, freq_side:, freq_side:]
    imag_part = second[:, :freq_side, freq_side:] + second[:, freq_side:, :freq_side]
    box_count = box_stack.shape[0]
    joined = jnp.concatenate([real_part.reshape(box_count, -1) * ctf_rows, imag_part.reshape(box_count, -1) * ctf_rows], axis=1)
    return joined.astype(jnp.bfloat16)

def shift_rows(window, cosine, sine_part, freq_side):
    box_count = window.shape[0]
    freq_area = freq_side * freq_side
    real_w = window[:, :freq_area].astype(jnp.float32)[:, None, :]
    imag_w = window[:, freq_area:].astype(jnp.float32)[:, None, :]
    real_s = real_w * cosine[None] - imag_w * sine_part[None]
    imag_s = real_w * sine_part[None] + imag_w * cosine[None]
    joined = jnp.concatenate([real_s, imag_s], axis=2).astype(jnp.bfloat16)
    return joined.reshape(box_count * cosine.shape[0], 2 * freq_area)

def reference(micrographs, mic_defocus, defocus, pick_list, template_bank, rot_index):
    total = P_DEV * N_DOM
    target_index = pick_list[3]
    column_count = target_index.shape[0]
    placed = jnp.where(target_index >= 0, target_index, total)
    row_of = jnp.zeros((total,), jnp.int32).at[placed].set(jnp.arange(column_count, dtype=jnp.int32), mode='drop')
    owner = (row_of // PICK_CAP).astype(jnp.int32)
    mic_global = (owner * MICS_DEV + pick_list[0][row_of]).astype(jnp.int32)
    top_rows = pick_list[1][row_of].astype(jnp.int32)
    left_cols = pick_list[2][row_of].astype(jnp.int32)
    defocus_ids = mic_defocus[mic_global]
    dft_table = forward_table(BOX, K)
    ctf_all = ctf_table(defocus, K)
    cosine, sine_part = shift_tables(BOX, K, SH)
    templates = template_bank[rot_index.reshape(-1)]

    def crop_one(mic_id, top_row, left_col):
        return lax.dynamic_slice(micrographs, (mic_id, top_row, left_col), (1, BOX, BOX))[0]

    def one_block(block_args):
        mic_b, top_b, left_b, id_b = block_args
        box_stack = jax.vmap(crop_one)(mic_b, top_b, left_b)
        window = spectra(box_stack, dft_table, ctf_all[id_b], K)
        shifted = shift_rows(window, cosine, sine_part, K)
        scores = jnp.dot(shifted, templates.T, preferred_element_type=jnp.float32).astype(jnp.bfloat16)
        return scores.reshape(P_DEV, SHIFTS, TEMPLATES)
    result = lax.map(one_block, (mic_global.reshape(N_DOM, P_DEV), top_rows.reshape(N_DOM, P_DEV), left_cols.reshape(N_DOM, P_DEV), defocus_ids.reshape(N_DOM, P_DEV)))
    return result.reshape(total, SHIFTS, TEMPLATES)
```

```python
import functools
import math

import jax
import jax.numpy as jnp
import ml_dtypes
import numpy as np
from jax import lax
from jax.experimental import pallas as pl
from jax.experimental.pallas import tpu as pltpu
from jax.sharding import PartitionSpec as P

BOX = 256
K = 32
HALF = K // 2
SH = 4
P_DEV = 96
SHIFTS = SH * SH
LANES = 128
ROWS = 16
STEP = 32
PER_BOX = BOX // STEP
GROUP = 4
CHUNK = 16
HALVES = 3
MAIN = K * K // 2
EXTRA = 64
AREA = 2 * (MAIN + EXTRA)

TWO_PI = 2.0 * math.pi
CHI_SCALE = 0.05
CHI_SHIFT = 0.1

MESH = pl.DeviceIdType.MESH
F32 = jnp.float32
BF16 = jnp.bfloat16


def bf(x):
    return np.asarray(x, np.float32).astype(ml_dtypes.bfloat16)


def turn(product):
    return TWO_PI * np.mod(product, BOX) / BOX


def row_order():
    return [4 * s + g - HALF for g in range(4) for s in range(4)]


def dft_tables():
    pixels = np.arange(BOX)
    scale = 1.0 / math.sqrt(BOX)
    order = np.array(row_order()).reshape(4, 4)
    cosine = np.cos(turn(order[..., None] * pixels)) * scale
    sine = -np.sin(turn(order[..., None] * pixels)) * scale
    rows = np.stack([cosine, sine], axis=1).reshape(K, BOX)
    left = np.zeros((PER_BOX * K + ROWS, 2 * BOX))
    for b in range(PER_BOX):
        span = slice(b * STEP, b * STEP + BOX)
        left[b * K : (b + 1) * K, span] = rows
        left[PER_BOX * K + b, span] = scale
    fix = np.zeros((K + ROWS, 2 * ROWS))
    fix[:K, :ROWS] = rows[:, :ROWS]
    fix[:K, ROWS:] = rows[:, -ROWS:]
    fix[K] = scale
    freq = np.arange(K) - HALF
    right = np.zeros((GROUP, BOX, 2, GROUP, K))
    for j in range(GROUP):
        right[j, :, 0, j] = np.cos(turn(freq[:, None] * pixels)).T * scale
        right[j, :, 1, j] = -np.sin(turn(freq[:, None] * pixels)).T * scale
    return bf(left), bf(fix), bf(right.reshape(GROUP * BOX, 2 * GROUP * K))


def swap_table():
    r = np.arange(ROWS)
    low = [(r < t).astype(float) for t in range(ROWS)]
    high = [-(r >= t).astype(float) for t in range(ROWS)]
    return bf(np.broadcast_to(np.array(low + high)[:, :, None], (2 * ROWS, ROWS, LANES)))


def phase_tables():
    sub, lane = np.arange(8)[:, None], np.arange(LANES)[None, :]
    t = np.arange(STEP)[:, None, None]
    t = np.where(t < ROWS, t, t - STEP)
    rows = turn(t * (4 * (sub % 4) + lane // K - HALF))
    edge = turn(t * (4 * (sub % 4) + lane % 4 - HALF))
    cols = turn(np.arange(LANES)[:, None] * (lane % K - HALF))
    far = turn(np.arange(ROWS)[:, None] * HALF + 0 * lane)
    return [f(x).astype(np.float32) for x in (rows, edge, cols, far) for f in (np.cos, np.sin)]


def fold_table():
    table = np.zeros((MAIN, MAIN + LANES))
    for f in range(MAIN):
        u, v = f // K - HALF, f % K - HALF
        if -u < HALF and -v < HALF:
            table[-u * K + HALF - v, f] = 1
    for lane in range(K):
        table[lane, MAIN + lane] = 1
    for lane in range(1, HALF):
        table[(HALF - lane) * K, MAIN + K + lane] = 1
    return bf(table)


def shift_phases():
    moves = np.arange(SH) - SH // 2
    row_move = np.repeat(moves, SH)[:, None]
    col_move = np.tile(moves, SH)[:, None]
    f = np.arange(MAIN)
    u, v = f // K - HALF, f % K - HALF
    lane = np.arange(EXTRA)
    low = lane < K
    u = np.concatenate([u, np.where(low, 0, lane - K - HALF)])
    v = np.concatenate([v, np.where(low, lane - HALF, HALF)])
    phase = turn(row_move * u + col_move * v)
    cosine, sine = np.cos(phase), np.sin(phase)
    main = [x[:, :MAIN].reshape(SHIFTS, MAIN // LANES, LANES).transpose(1, 0, 2) for x in (cosine, sine)]
    last_c = np.concatenate([cosine[:, MAIN:]] * 2, axis=1)
    last_s = np.concatenate([-sine[:, MAIN:], sine[:, MAIN:]], axis=1)
    return [
        np.concatenate([m, x[None]]).astype(np.float32) for m, x in zip(main, (last_c, last_s), strict=True)
    ]


def spread_tables(slot_cap):
    groups = slot_cap // GROUP
    lane = np.arange(LANES)
    edge = np.zeros((ROWS, LANES))
    flat = np.zeros((ROWS, LANES))
    for i in range(slot_cap):
        q, j = i // GROUP, i % GROUP
        edge[i] = (lane // K == j) & (lane % K // 4 == q)
        flat[i] = lane // K == j
    gather = np.zeros((10, LANES, LANES))
    for s in range(8):
        gather[s, lane, EXTRA * (s // 4) + K + 4 * (s % 4) + lane % 4] = 1
    for part in range(2):
        gather[8 + part, lane, EXTRA * part + lane % K] = 1
    assert 8 + 2 * groups < ROWS and groups * 4 <= K
    return bf(edge), bf(flat), bf(gather.reshape(10 * LANES, LANES))


def bits(n):
    return (n - 1).bit_length()


def flip(x):
    return pltpu.roll(x, 4, 0)


def chain(ids, values):
    total = values[0]
    for i, value in enumerate(values[1:], 1):
        total = jnp.where(ids == i, value, total)
    return total


def crop_kernel(peers, slot_cap, shifts, bank_rows, info, mic_def, defocus, shard, mic_h, left_h, fix_h, right_h, swap_h,
                prow_ch, prow_sh, edge_ch, edge_sh, pcol_ch, pcol_sh, far_ch, far_sh, fold_h, arrived, bank,
                mic, left_t, fix_t, right_t, swap_t, prow_c, prow_s, edge_c, edge_s, pcol_c, pcol_s, far_c, far_s, fold_t,
                aligned, flat, ctf, lhs, padded, outgoing, load_sem, send_sem, recv_sem, local_sem, bank_send, bank_recv):
    groups = slot_cap // GROUP
    depth = peers // 4
    mics, blocks, tiles_high = mic.shape[:3]
    me = lax.axis_index("dom")
    my_z, my_y, my_c = me // 4, (me // 2) % 2, me % 2
    label_bits, row_bits, col_bits = shifts

    tables = [
        pltpu.make_async_copy(src, dst, load_sem.at[i])
        for i, (src, dst) in enumerate(
            [(fold_h, fold_t), (left_h, left_t), (fix_h, fix_t), (right_h, right_t), (swap_h, swap_t),
             (prow_ch, prow_c), (prow_sh, prow_s), (edge_ch, edge_c), (edge_sh, edge_s),
             (pcol_ch, pcol_c), (pcol_sh, pcol_s), (far_ch, far_c), (far_sh, far_s)])
    ]

    def load(m, b):
        return pltpu.make_async_copy(
            mic_h.at[m, :, :, pl.ds(b * LANES, LANES)], mic.at[m, b], load_sem.at[len(tables) + m * blocks + b])

    tables[0].start()
    tables[1].start()
    for m in range(mics):
        for b in range(blocks):
            load(m, b).start()
    for table in tables[2:]:
        table.start()

    barrier = pltpu.get_barrier_semaphore()

    def greet(k, carry):
        pl.semaphore_signal(barrier, inc=1, device_id={"dom": (me + k) % peers}, device_id_type=MESH)
        return carry

    lax.fori_loop(1, peers, greet, 0)

    sub = lax.broadcasted_iota(jnp.int32, (8, LANES), 0)
    lane = lax.broadcasted_iota(jnp.int32, (8, LANES), 1)
    sign = jnp.where(sub < 4, -1.0, 1.0).astype(F32)
    lane_u = 4 * (sub % 4) - HALF
    planes = [
        (lane_u + lane // K, lane % K - HALF),
        (lane_u + lane % 4, 0 * lane + HALF),
        (0 * lane, lane % K - HALF),
    ]
    for m in range(mics):
        value = defocus[mic_def[m]]
        for i, (u, v) in enumerate(planes):
            radius = (u * u + v * v).astype(F32)
            weight = -jnp.sin(CHI_SCALE * value * radius + CHI_SHIFT)
            ctf[m, 2 * i] = weight
            ctf[m, 2 * i + 1] = weight * sign

    tables[0].wait()
    half = shard.shape[1] // 4
    upper = jnp.concatenate([shard[:, half : 2 * half], shard[:, 3 * half :]], axis=0)
    folded = jnp.dot(upper, fold_t[...], preferred_element_type=F32)
    rows = shard.shape[0]
    re, im = folded[:rows], folded[rows:]
    last_lane = lax.broadcasted_iota(jnp.int32, (rows, EXTRA), 1)
    im_last = jnp.where(last_lane < K, im[:, half : half + EXTRA], -im[:, half : half + EXTRA])
    padded[...] = jnp.zeros_like(padded)
    padded[:rows] = jnp.concatenate(
        [shard[:, :half].astype(F32) + re[:, :half], shard[:, 2 * half : 3 * half].astype(F32) - im[:, :half],
         re[:, half : half + EXTRA], im_last], axis=1).astype(BF16)

    lane_id = lax.broadcasted_iota(jnp.int32, (ROWS, LANES), 1).astype(F32).astype(BF16)
    row_id = lax.broadcasted_iota(jnp.int32, (ROWS, LANES), 0)
    label_lane = lax.broadcasted_iota(jnp.int32, (8, LANES), 1)
    which = lane // K
    edge_id = (lane % K) // 4 * GROUP + lane // K
    pl.semaphore_wait(barrier, peers - 1)

    def to_z(d):
        there = (my_z + d) % depth
        return pltpu.make_async_remote_copy(
            src_ref=padded, dst_ref=bank.at[me], send_sem=bank_send.at[d], recv_sem=bank_recv.at[d],
            device_id={"dom": there * 4 + me % 4}, device_id_type=MESH)

    def to_y(i):
        row = i * 4 + me % 4
        return pltpu.make_async_remote_copy(
            src_ref=bank.at[row], dst_ref=bank.at[row], send_sem=bank_send.at[depth + i],
            recv_sem=bank_recv.at[depth + i],
            device_id={"dom": my_z * 4 + (1 - my_y) * 2 + my_c}, device_id_type=MESH)

    def to_c(i):
        row = i * 2 + my_c
        return pltpu.make_async_remote_copy(
            src_ref=bank.at[row], dst_ref=bank.at[row], send_sem=bank_send.at[2 * depth + i],
            recv_sem=bank_recv.at[2 * depth + i],
            device_id={"dom": my_z * 4 + my_y * 2 + 1 - my_c}, device_id_type=MESH)

    def each(count, act, first=0):
        def step(i, carry):
            act(i)
            return carry

        lax.fori_loop(first, count, step, 0)

    own = pltpu.make_async_copy(padded, bank.at[me], local_sem.at[0])
    own.start()
    each(depth, lambda d: to_z(d).start(), 1)

    tables[1].wait()
    per = BOX // ROWS
    chunks = tiles_high // per

    def align(step, carry):
        m, b = step // (blocks // 2), step % (blocks // 2) * 2
        load(m, b).wait()
        load(m, b + 1).wait()
        sums = []

        def pixels(first, count):
            return jnp.concatenate(
                [mic[m, b + h, pl.ds(first, count)].reshape(count * ROWS, LANES) for h in range(2)], axis=1)

        def keep(n, x):
            for t in range(2):
                for h in range(2):
                    aligned[m, n, t, b + h] = x[t * ROWS : (t + 1) * ROWS, h * LANES : (h + 1) * LANES].astype(BF16)

        for a in range(chunks - 1):
            x = jnp.dot(left_t[...], pixels(a * per, 2 * per), preferred_element_type=F32)
            for n in range(PER_BOX):
                keep(a * PER_BOX + n, x[n * K : (n + 1) * K])
            sums.append(x[PER_BOX * K : PER_BOX * K + PER_BOX])
        end = pixels((chunks - 1) * per, per)
        keep((chunks - 1) * PER_BOX, jnp.dot(left_t[:K, :BOX], end, preferred_element_type=F32))
        x = jnp.dot(left_t[PER_BOX * K :, :BOX], end, preferred_element_type=F32)
        sums.append(x[:PER_BOX])
        for t in range(chunks // 2):
            pair = jnp.concatenate([sums[2 * t], sums[2 * t + 1]], axis=0).astype(BF16)
            for h in range(2):
                flat[m, t, b + h] = pair[:, h * LANES : (h + 1) * LANES]
        return carry

    lax.fori_loop(0, mics * blocks // 2, align, 0)
    for table in tables[2:]:
        table.wait()

    def peer_of(k):
        step = k // 4
        dz = jnp.where(step < depth // 2, depth // 2 + step, depth - 1 - step)
        return ((my_z + dz) % depth) * 4 + (me + 1 + k) % 4

    def block_copy(k):
        return pltpu.make_async_remote_copy(
            src_ref=outgoing.at[k], dst_ref=arrived.at[me], send_sem=send_sem.at[k], recv_sem=recv_sem.at[k],
            device_id={"dom": peer_of(k)}, device_id_type=MESH)

    def unpack(at):
        packed = lax.shift_right_logical(info[at], label_bits)
        left = packed & (2**col_bits - 1)
        top = lax.shift_right_logical(packed, col_bits) & (2**row_bits - 1)
        return lax.shift_right_logical(packed, col_bits + row_bits), top, left

    def gather(q, j, box):
        m, top, left = box
        block, rl = lax.shift_right_logical(left, 7), left & (LANES - 1)
        third = jnp.minimum(block + 2, blocks - 1)
        window = lax.shift_right_logical(top + ROWS, 5)
        tile = lax.shift_right_logical(top, 4)
        end_tile = jnp.minimum(tile + per, tiles_high - 1)
        mask = lane_id >= rl.astype(F32).astype(BF16)
        coef = swap_t[top & (STEP - 1)]

        def put(t, read):
            rows = pl.ds(q * 4 * ROWS + t * ROWS, ROWS)
            lhs[rows, pl.ds(2 * j * LANES, LANES)] = jnp.where(mask, read(block), read(third))
            lhs[rows, pl.ds((2 * j + 1) * LANES, LANES)] = read(block + 1)

        put(0, lambda b: aligned[m, window, 0, b])
        put(1, lambda b: aligned[m, window, 1, b])
        put(2, lambda b: flat[m, lax.shift_right_logical(window, 4), b])
        put(3, lambda b: (mic[m, b, end_tile] - mic[m, b, tile]) * coef)

    def per_peer(k, carry):
        base = peer_of(k) * slot_cap
        boxes = [unpack(base + i) for i in range(slot_cap)]
        for i, box in enumerate(boxes):
            gather(i // GROUP, i % GROUP, box)

        @pl.when(k > 0)
        def _():
            block_copy(k - 1).start()

        @pl.when(k == peers // 3)
        def _():
            own.wait()
            each(depth, lambda d: to_z(d).wait(), 1)
            each(depth, lambda i: to_y(i).start())

        @pl.when(k == peers - 2)
        def _():
            each(depth, lambda i: to_y(i).wait())
            each(2 * depth, lambda i: to_c(i).start())

        first = jnp.dot(lhs[...], right_t[...], preferred_element_type=F32)
        fixes = []
        for q in range(groups):
            part = first[(q * 4 + 3) * ROWS : (q * 4 + 4) * ROWS]
            odd = chain(which[:1], [(boxes[q * GROUP + j][1] >> 4) & 1 for j in range(GROUP)])
            odd = jnp.concatenate([odd, odd], axis=1) == 1
            fixes.append(jnp.concatenate([jnp.where(odd, 0.0, part), jnp.where(odd, part, 0.0)], axis=0).astype(BF16))
        fixed = jnp.dot(fix_t[...], jnp.concatenate(fixes, axis=1), preferred_element_type=F32)

        far = None
        flats = [jnp.zeros((8, LANES), F32)]
        tiles = []
        for q in range(groups):
            add = fixed[:, q * 2 * LANES : (q + 1) * 2 * LANES]
            top_rows = q * 4 * ROWS
            values, others = [], []
            for g in range(4):
                x = first[top_rows + 8 * g : top_rows + 8 * g + 8] + add[8 * g : 8 * g + 8]
                cos_part, sin_part = x[:, :LANES], flip(x[:, LANES:]) * sign
                values.append(cos_part + sin_part)
                others.append(cos_part - sin_part)
            mine = boxes[q * GROUP : (q + 1) * GROUP]
            edge = None
            for g in range(4):
                piece = pltpu.roll(others[g], g, 1) if g else others[g]
                edge = piece if edge is None else jnp.where(lane % 4 == g, piece, edge)
            edge = pltpu.roll(edge, 4 * q, 1) if q else edge
            far = edge if far is None else jnp.where(edge_id // GROUP == q, edge, far)

            at = chain(which[:1], [(lax.shift_right_logical(b[1] + ROWS, 5)) & (ROWS - 1) for b in mine])
            at = jnp.concatenate([at, at], axis=1)
            sums = first[top_rows + 2 * ROWS : top_rows + 3 * ROWS]
            rows16 = lax.broadcasted_iota(jnp.int32, (ROWS, 2 * LANES), 0)
            line = jnp.sum(jnp.where(rows16 == at, sums, 0.0), axis=0, keepdims=True) + add[K : K + 1]
            re, im = line[:, :LANES], line[:, LANES:]
            rls = [b[2] & (LANES - 1) for b in mine]
            cv = chain(which[:1], [pcol_c[pl.ds(rl, 1), :] for rl in rls])
            sv = chain(which[:1], [pcol_s[pl.ds(rl, 1), :] for rl in rls])
            weight = chain(which[:1], [ctf[b[0], 4, :1] for b in mine])
            out_re, out_im = (re * cv - im * sv) * weight, (re * sv + im * cv) * weight
            flats = [jnp.where(sub == q, out_re, jnp.where(sub == groups + q, out_im, flats[0]))]

            for j, (m, top, left) in enumerate(mine):
                total = None
                for g in range(4):
                    shift = (K * (g - j)) % LANES
                    piece = pltpu.roll(values[g], shift, 1) if shift else values[g]
                    total = piece if total is None else jnp.where(which == g, piece, total)
                rt, rl = top & (STEP - 1), left & (LANES - 1)
                cu, su = prow_c[rt], prow_s[rt]
                cv, sv = pcol_c[pl.ds(rl, 1), :], pcol_s[pl.ds(rl, 1), :]
                a = (cu * cv - su * sv) * ctf[m, 0]
                b = (su * cv + cu * sv) * ctf[m, 1]
                tiles.append(total * a + flip(total) * b)
        for i in range(slot_cap // 2):
            outgoing[k, i] = jnp.concatenate([tiles[2 * i], tiles[2 * i + 1]], axis=0).astype(BF16)

        rts = [b[1] & (STEP - 1) for b in boxes]
        ends = [b[2] & (ROWS - 1) for b in boxes]
        cu, su = chain(edge_id, [edge_c[rt] for rt in rts]), chain(edge_id, [edge_s[rt] for rt in rts])
        ce = chain(edge_id, [far_c[pl.ds(e, 1), :] for e in ends])
        se = chain(edge_id, [far_s[pl.ds(e, 1), :] for e in ends])
        weight = chain(edge_id, [ctf[b[0], 2] for b in boxes])
        far = far * (cu * ce - su * se) * weight + flip(far) * (su * ce + cu * se) * weight * sign
        labels = jnp.zeros((8, LANES), jnp.int32)
        for i in range(slot_cap):
            labels = jnp.where(label_lane == (info[base + i] & (2**label_bits - 1)) - 1, i + 1, labels)
        low = jnp.where(sub == 2 * groups, labels.astype(F32), flats[0])
        outgoing[k, slot_cap // 2] = jnp.concatenate([far, low], axis=0).astype(BF16)
        return carry

    lax.fori_loop(0, peers, per_peer, 0)
    mine = pltpu.make_async_copy(outgoing.at[peers - 1], arrived.at[me], local_sem.at[1])
    mine.start()
    each(2 * depth, lambda i: to_c(i).wait())
    each(peers - 1, lambda k: block_copy(k).wait())
    mine.wait()


def score_kernel(groups, tiles, where, arrived, bank, pick, cos_t, sin_t, edge_t, flat_t, gather_t, out, spread, extras, *halves):
    base = pl.program_id(0) * CHUNK * len(halves)
    peers = arrived.shape[0] // tiles

    @pl.when(pl.program_id(0) == 0)
    def _():
        row = lax.broadcasted_iota(jnp.int32, (ROWS, LANES), 0) // GROUP

        def one(p, carry):
            x = arrived[p * tiles + tiles - 1].astype(F32)
            at = pl.ds(pl.multiple_of(p * ROWS, ROWS), ROWS)

            def line(s):
                return jnp.broadcast_to(x[s : s + 1], (ROWS, LANES))

            for s in range(8):
                spread[at, s * LANES : (s + 1) * LANES] = line(s).astype(BF16) * edge_t[...]
            for part in range(2):
                rows = chain(row, [line(8 + part * groups + q) for q in range(groups)])
                spread[at, (8 + part) * LANES : (9 + part) * LANES] = rows.astype(BF16) * flat_t[...]
            return carry

        lax.fori_loop(0, peers, one, 0)
        extras[...] = jnp.dot(spread[...], gather_t[...], preferred_element_type=F32)

    def expand(half, lhs):
        for n in range(CHUNK):
            slot = where[base + half * CHUNK + n]
            p, i = lax.shift_right_logical(slot, 4), slot & (ROWS - 1)
            pair = arrived[p * tiles + lax.shift_right_logical(i, 1)].astype(F32)
            x = jnp.where((i & 1) == 1, pair[8:], pair[:8])
            rows = slice(n * SHIFTS, (n + 1) * SHIFTS)
            for k in range(4):
                re = jnp.broadcast_to(x[k : k + 1], (SHIFTS, LANES))
                im = jnp.broadcast_to(x[4 + k : 5 + k], (SHIFTS, LANES))
                c, s = cos_t[k], sin_t[k]
                lhs[rows, k * LANES : (k + 1) * LANES] = (re * c - im * s).astype(BF16)
                lhs[rows, (4 + k) * LANES : (5 + k) * LANES] = (re * s + im * c).astype(BF16)
            x = jnp.broadcast_to(extras[pl.ds(slot, 1), :], (SHIFTS, LANES))
            turned = jnp.broadcast_to(pltpu.roll(jnp.broadcast_to(extras[pl.ds(slot, 1), :], (8, LANES)), EXTRA, 1)[:1],
                                      (SHIFTS, LANES))
            lhs[rows, 8 * LANES :] = (x * cos_t[4] + turned * sin_t[4]).astype(BF16)

    def score(lhs):
        return lax.dot_general(lhs[...], bank[...], (((1,), (1,)), ((), ())),
                               preferred_element_type=F32).astype(BF16)

    def emit(half, scores):
        rows = CHUNK * SHIFTS
        picked = jnp.dot(scores, pick[...], preferred_element_type=F32)
        out[half * rows : (half + 1) * rows] = picked.astype(BF16)

    waiting = None
    for half, lhs in enumerate(halves):
        expand(half, lhs)
        scores = score(lhs)
        if waiting is not None:
            emit(half - 1, waiting)
        waiting = scores
    emit(len(halves) - 1, waiting)


VMEM = pl.BlockSpec(memory_space=pltpu.VMEM)
HBM = pl.BlockSpec(memory_space=pltpu.HBM)
ANY = pl.BlockSpec(memory_space=pl.ANY)
SMEM = pl.BlockSpec(memory_space=pltpu.SMEM)


def body(micrographs, mic_defocus, defocus, pick_list, template_bank, rot_index):
    peers = lax.axis_size("dom")
    slot_cap = (P_DEV + peers - 1) // peers * 2
    slot_cap = -(-slot_cap // GROUP) * GROUP
    groups = slot_cap // GROUP
    mics, height, width = micrographs.shape
    label_bits, row_bits, col_bits = bits(P_DEV + 1), bits(height), bits(width)
    columns = pick_list.shape[1]

    target = pick_list[3]
    live = target >= 0
    target_dev = jnp.where(live, target // P_DEV, -1)
    label = jnp.where(live, jnp.mod(target, P_DEV) + 1, 0)
    ids = jnp.arange(columns, dtype=jnp.int32)
    earlier = (ids[None, :] < ids[:, None]) & (target_dev[None, :] == target_dev[:, None])
    rank = jnp.sum(earlier.astype(jnp.int32), axis=1)
    position = jnp.where(live, target_dev * slot_cap + rank, -1)
    mic_id = jnp.clip(pick_list[0], 0, mics - 1)
    top = jnp.clip(pick_list[1], 0, height - BOX)
    left = jnp.clip(pick_list[2], 0, width - BOX)
    packed = (((mic_id << row_bits) + top << col_bits) + left << label_bits) + label
    slots = jnp.arange(peers * slot_cap, dtype=jnp.int32)
    info = jnp.sum(jnp.where(position[None, :] == slots[:, None], packed[None, :], 0), axis=1)

    left_t, fix_t, right_t = dft_tables()
    tables = [left_t, fix_t, right_t, swap_table()] + phase_tables() + [fold_table()]
    bank_rows = template_bank.shape[0]
    pad_rows = -(-bank_rows // ROWS) * ROWS
    copies = len(tables) + mics * (width // LANES)
    tiles = slot_cap // 2 + 1
    windows = (height - BOX) // STEP + 1
    dma = pltpu.SemaphoreType.DMA
    arrived, bank = pl.pallas_call(
        functools.partial(crop_kernel, peers, slot_cap, (label_bits, row_bits, col_bits), bank_rows),
        out_shape=(
            jax.ShapeDtypeStruct((peers, tiles, ROWS, LANES), BF16),
            jax.ShapeDtypeStruct((peers, pad_rows, AREA), BF16),
        ),
        in_specs=[SMEM, SMEM, SMEM, VMEM] + [HBM] * (1 + len(tables)),
        out_specs=(ANY, ANY),
        scratch_shapes=[
            pltpu.VMEM((mics, width // LANES, height // ROWS, ROWS, LANES), BF16),
            *[pltpu.VMEM(t.shape, t.dtype) for t in tables],
            pltpu.VMEM((mics, windows, 2, width // LANES, ROWS, LANES), BF16),
            pltpu.VMEM((mics, height // (2 * BOX), width // LANES, ROWS, LANES), BF16),
            pltpu.VMEM((mics, 6, 8, LANES), F32),
            pltpu.VMEM((groups * 4 * ROWS, GROUP * BOX), BF16),
            pltpu.VMEM((pad_rows, AREA), BF16),
            pltpu.VMEM((peers, tiles, ROWS, LANES), BF16),
            dma((copies,)), dma((peers,)), dma((peers,)), dma((2,)), dma((peers,)), dma((peers,)),
        ],
        compiler_params=pltpu.CompilerParams(
            collective_id=0, has_side_effects=True, vmem_limit_bytes=56 << 20),
        name="crop",
    )(info, mic_defocus, defocus, template_bank,
      micrographs.reshape(mics, height // ROWS, ROWS, width), *[jnp.asarray(t) for t in tables])
    bank = bank.reshape(peers * pad_rows, AREA)

    got = arrived[:, tiles - 1, 8 + 2 * groups, :P_DEV].astype(jnp.int32)
    at = jnp.arange(peers, dtype=jnp.int32)[:, None] * ROWS - 1
    where = jnp.sum(jnp.where(got > 0, got + at, 0), axis=0)

    flat = rot_index.reshape(-1)
    entry = flat + lax.div(flat, jnp.int32(bank_rows)) * (pad_rows - bank_rows)
    templates = flat.shape[0]
    pick = (jnp.arange(peers * pad_rows, dtype=jnp.int32)[:, None] == entry[None, :]).astype(BF16)

    consts = shift_phases() + list(spread_tables(slot_cap))
    full = lambda shape: pl.BlockSpec(shape, lambda i: (0,) * len(shape), pipeline_mode=pl.Buffered(1))
    out = pl.pallas_call(
        functools.partial(score_kernel, groups, tiles),
        grid=(P_DEV // (HALVES * CHUNK),),
        out_shape=jax.ShapeDtypeStruct((P_DEV * SHIFTS, templates), BF16),
        in_specs=[
            SMEM,
            full((peers * tiles, ROWS, LANES)),
            full((peers * pad_rows, AREA)),
            full((peers * pad_rows, templates)),
            *[full(c.shape) for c in consts],
        ],
        out_specs=pl.BlockSpec((HALVES * CHUNK * SHIFTS, templates), lambda i: (i, 0)),
        scratch_shapes=[pltpu.VMEM((peers * ROWS, 10 * LANES), BF16), pltpu.VMEM((peers * ROWS, LANES), F32)]
        + [pltpu.VMEM((CHUNK * SHIFTS, AREA), BF16)] * HALVES,
        compiler_params=pltpu.CompilerParams(vmem_limit_bytes=56 << 20),
        name="score",
    )(where, arrived.reshape(peers * tiles, ROWS, LANES), bank, pick, *[jnp.asarray(c) for c in consts])
    return out.reshape(P_DEV, SHIFTS, templates)


def solution(mesh):
    return jax.shard_map(
        body,
        mesh=mesh,
        in_specs=(
            P(("groups", "dom"), None, None),
            P(("groups", "dom")),
            P("groups"),
            P(None, ("groups", "dom")),
            P(("groups", "dom"), None),
            P("groups", None),
        ),
        out_specs=P(("groups", "dom"), None, None),
        check_vma=False,
    )
```

```python
import functools
import math

import jax
import jax.numpy as jnp
import ml_dtypes
import numpy as np
from jax import lax
from jax.experimental import pallas as pl
from jax.experimental.pallas import tpu as pltpu
from jax.sharding import PartitionSpec as P

BOX = 256
K = 32
HALF = K // 2
SH = 4
P_DEV = 96
SHIFTS = SH * SH
LANES = 128
ROWS = 16
STEP = 32
PER_BOX = BOX // STEP
GROUP = 4
CHUNK = 16
HALVES = 3
MAIN = K * K // 2
EXTRA = 64
AREA = 2 * (MAIN + EXTRA)

TWO_PI = 2.0 * math.pi
CHI_SCALE = 0.05
CHI_SHIFT = 0.1

MESH = pl.DeviceIdType.MESH
F32 = jnp.float32
BF16 = jnp.bfloat16


def bf(x):
    return np.asarray(x, np.float32).astype(ml_dtypes.bfloat16)


def turn(product):
    return TWO_PI * np.mod(product, BOX) / BOX


def row_order():
    return [4 * s + g - HALF for g in range(4) for s in range(4)]


def dft_tables():
    pixels = np.arange(BOX)
    scale = 1.0 / math.sqrt(BOX)
    order = np.array(row_order()).reshape(4, 4)
    cosine = np.cos(turn(order[..., None] * pixels)) * scale
    sine = -np.sin(turn(order[..., None] * pixels)) * scale
    rows = np.stack([cosine, sine], axis=1).reshape(K, BOX)
    left = np.zeros((PER_BOX * K + ROWS, 2 * BOX))
    for b in range(PER_BOX):
        span = slice(b * STEP, b * STEP + BOX)
        left[b * K : (b + 1) * K, span] = rows
        left[PER_BOX * K + b, span] = scale
    fix = np.zeros((K + ROWS, 2 * ROWS))
    fix[:K, :ROWS] = rows[:, :ROWS]
    fix[:K, ROWS:] = rows[:, -ROWS:]
    fix[K] = scale
    freq = np.arange(K) - HALF
    right = np.zeros((GROUP, BOX, 2, GROUP, K))
    for j in range(GROUP):
        right[j, :, 0, j] = np.cos(turn(freq[:, None] * pixels)).T * scale
        right[j, :, 1, j] = -np.sin(turn(freq[:, None] * pixels)).T * scale
    return bf(left), bf(fix), bf(right.reshape(GROUP * BOX, 2 * GROUP * K))


def swap_table():
    r = np.arange(ROWS)
    low = [(r < t).astype(float) for t in range(ROWS)]
    high = [-(r >= t).astype(float) for t in range(ROWS)]
    return bf(np.broadcast_to(np.array(low + high)[:, :, None], (2 * ROWS, ROWS, LANES)))


def phase_tables():
    sub, lane = np.arange(8)[:, None], np.arange(LANES)[None, :]
    t = np.arange(STEP)[:, None, None]
    t = np.where(t < ROWS, t, t - STEP)
    rows = turn(t * (4 * (sub % 4) + lane // K - HALF))
    edge = turn(t * (4 * (sub % 4) + lane % 4 - HALF))
    cols = turn(np.arange(LANES)[:, None] * (lane % K - HALF))
    far = turn(np.arange(ROWS)[:, None] * HALF + 0 * lane)
    return [f(x).astype(np.float32) for x in (rows, edge, cols, far) for f in (np.cos, np.sin)]


def fold_table():
    table = np.zeros((MAIN, MAIN + LANES))
    for f in range(MAIN):
        u, v = f // K - HALF, f % K - HALF
        if -u < HALF and -v < HALF:
            table[-u * K + HALF - v, f] = 1
    for lane in range(K):
        table[lane, MAIN + lane] = 1
    for lane in range(1, HALF):
        table[(HALF - lane) * K, MAIN + K + lane] = 1
    return bf(table)


def shift_phases():
    moves = np.arange(SH) - SH // 2
    row_move = np.repeat(moves, SH)[:, None]
    col_move = np.tile(moves, SH)[:, None]
    f = np.arange(MAIN)
    u, v = f // K - HALF, f % K - HALF
    lane = np.arange(EXTRA)
    low = lane < K
    u = np.concatenate([u, np.where(low, 0, lane - K - HALF)])
    v = np.concatenate([v, np.where(low, lane - HALF, HALF)])
    phase = turn(row_move * u + col_move * v)
    cosine, sine = np.cos(phase), np.sin(phase)
    main = [x[:, :MAIN].reshape(SHIFTS, MAIN // LANES, LANES).transpose(1, 0, 2) for x in (cosine, sine)]
    last_c = np.concatenate([cosine[:, MAIN:]] * 2, axis=1)
    last_s = np.concatenate([-sine[:, MAIN:], sine[:, MAIN:]], axis=1)
    return [
        np.concatenate([m, x[None]]).astype(np.float32) for m, x in zip(main, (last_c, last_s), strict=True)
    ]


def spread_tables(slot_cap):
    groups = slot_cap // GROUP
    lane = np.arange(LANES)
    edge = np.zeros((ROWS, LANES))
    flat = np.zeros((ROWS, LANES))
    for i in range(slot_cap):
        q, j = i // GROUP, i % GROUP
        edge[i] = (lane // K == j) & (lane % K // 4 == q)
        flat[i] = lane // K == j
    gather = np.zeros((10, LANES, LANES))
    for s in range(8):
        gather[s, lane, EXTRA * (s // 4) + K + 4 * (s % 4) + lane % 4] = 1
    for part in range(2):
        gather[8 + part, lane, EXTRA * part + lane % K] = 1
    assert 8 + 2 * groups < ROWS and groups * 4 <= K
    return bf(edge), bf(flat), bf(gather.reshape(10 * LANES, LANES))


def bits(n):
    return (n - 1).bit_length()


def flip(x):
    return pltpu.roll(x, 4, 0)


def chain(ids, values):
    total = values[0]
    for i, value in enumerate(values[1:], 1):
        total = jnp.where(ids == i, value, total)
    return total


def crop_kernel(peers, slot_cap, shifts, pick_h, mic_def_h, defocus_h, shard_h, mic_h, left_h, fix_h, right_h, swap_h,
                prow_ch, prow_sh, edge_ch, edge_sh, pcol_ch, pcol_sh, far_ch, far_sh, fold_h, arrived, bank,
                mic, left_t, fix_t, right_t, swap_t, prow_c, prow_s, edge_c, edge_s, pcol_c, pcol_s, far_c, far_s, fold_t,
                info, info_v, mic_def, defocus, pick_v, shard, labels, aligned, flat, ctf, lhs_a, lhs_b, padded, outgoing, load_sem, send_sem, recv_sem, local_sem, bank_send, bank_recv, small_sem):
    groups = slot_cap // GROUP
    depth = peers // 4
    mics, blocks, tiles_high = mic.shape[0], mic.shape[1] - 1, mic.shape[2] - 1
    me = lax.axis_index("dom")
    my_z, my_y, my_c = me // 4, (me // 2) % 2, me % 2
    row_bits, col_bits = shifts

    tables = [
        pltpu.make_async_copy(src, dst, load_sem.at[i])
        for i, (src, dst) in enumerate(
            [(fold_h, fold_t), (left_h, left_t), (fix_h, fix_t), (right_h, right_t), (swap_h, swap_t),
             (prow_ch, prow_c), (prow_sh, prow_s), (edge_ch, edge_c), (edge_sh, edge_s),
             (pcol_ch, pcol_c), (pcol_sh, pcol_s), (far_ch, far_c), (far_sh, far_s)])
    ]

    def load(m, b):
        return pltpu.make_async_copy(
            mic_h.at[m, :, :, pl.ds(b * LANES, LANES)], mic.at[m, b, pl.ds(0, tiles_high)], load_sem.at[len(tables) + m * blocks + b])

    smalls = [
        pltpu.make_async_copy(src, dst, small_sem.at[i])
        for i, (src, dst) in enumerate(
            [(pick_h, pick_v), (mic_def_h, mic_def), (defocus_h, defocus), (shard_h, shard)])
    ]
    for small in smalls:
        small.start()
    tables[0].start()
    tables[1].start()
    for m in range(mics):
        for b in range(blocks):
            load(m, b).start()
    for table in tables[2:]:
        table.start()

    barrier = pltpu.get_barrier_semaphore()

    def greet(k, carry):
        pl.semaphore_signal(barrier, inc=1, device_id={"dom": (me + k) % peers}, device_id_type=MESH)
        return carry

    lax.fori_loop(1, peers, greet, 0)

    smalls[0].wait()
    columns = pick_v.shape[1]
    wide = -(-columns // LANES) * LANES
    picks = pick_v[...]
    if wide > columns:
        picks = jnp.concatenate([picks, jnp.full((picks.shape[0], wide - columns), -1, jnp.int32)], axis=1)
    height, width = mic_h.shape[1] * ROWS, mic_h.shape[3]
    spot = (jnp.clip(picks[:1], 0, mics - 1) << row_bits) + jnp.clip(picks[1:2], 0, height - BOX)
    spot = (spot << col_bits) + jnp.clip(picks[2:3], 0, width - BOX)
    target = picks[3:]
    device = target * (-(-(1 << 22) // P_DEV)) >> 22
    label = target - device * P_DEV
    chosen = lax.broadcasted_iota(jnp.int32, (peers, wide), 0) == device
    pick_lane = lax.broadcasted_iota(jnp.int32, (peers, wide), 1)
    rank = chosen.astype(jnp.int32)
    for power in range((wide - 1).bit_length()):
        rank = rank + jnp.where(pick_lane >= 1 << power, pltpu.roll(rank, 1 << power, 1), 0)
    rank = jnp.where(chosen, rank, 0)
    slot_lane = lax.broadcasted_iota(jnp.int32, (peers, LANES), 1)
    spots = jnp.zeros((peers, LANES), jnp.int32)
    for i in range(slot_cap):
        here = jnp.sum(jnp.where(rank == i + 1, spot, 0), axis=1, keepdims=True)
        spots = jnp.where(slot_lane == i, here, spots)
    info_v[...] = spots
    info_copy = pltpu.make_async_copy(info_v, info, small_sem.at[4])
    info_copy.start()
    named = lax.broadcasted_iota(jnp.int32, (LANES, wide), 0) == label
    labels[...] = lax.dot_general(
        rank.astype(F32).astype(BF16), jnp.where(named, 1.0, 0.0).astype(BF16),
        (((1,), (1,)), ((), ())), preferred_element_type=F32)

    smalls[1].wait()
    smalls[2].wait()
    sub = lax.broadcasted_iota(jnp.int32, (8, LANES), 0)
    lane = lax.broadcasted_iota(jnp.int32, (8, LANES), 1)
    sign = jnp.where(sub < 4, -1.0, 1.0).astype(F32)
    lane_u = 4 * (sub % 4) - HALF
    planes = [
        (lane_u + lane // K, lane % K - HALF),
        (lane_u + lane % 4, 0 * lane + HALF),
        (0 * lane, lane % K - HALF),
    ]
    for m in range(mics):
        value = defocus[mic_def[m]]
        for i, (u, v) in enumerate(planes):
            radius = (u * u + v * v).astype(F32)
            weight = -jnp.sin(CHI_SCALE * value * radius + CHI_SHIFT)
            ctf[m, 2 * i] = weight
            ctf[m, 2 * i + 1] = weight * sign

    tables[0].wait()
    smalls[3].wait()
    half = shard.shape[1] // 4
    upper = jnp.concatenate([shard[:, half : 2 * half], shard[:, 3 * half :]], axis=0)
    folded = jnp.dot(upper, fold_t[...], preferred_element_type=F32)
    rows = shard.shape[0]
    re, im = folded[:rows], folded[rows:]
    last_lane = lax.broadcasted_iota(jnp.int32, (rows, EXTRA), 1)
    im_last = jnp.where(last_lane < K, im[:, half : half + EXTRA], -im[:, half : half + EXTRA])
    padded[...] = jnp.zeros_like(padded)
    padded[:rows] = jnp.concatenate(
        [shard[:, :half].astype(F32) + re[:, :half], shard[:, 2 * half : 3 * half].astype(F32) - im[:, :half],
         re[:, half : half + EXTRA], im_last], axis=1).astype(BF16)

    for m in range(mics):
        for b in range(blocks + 1):
            mic[m, b, tiles_high] = jnp.zeros((ROWS, LANES), BF16)

    lane_id = lax.broadcasted_iota(jnp.int32, (ROWS, LANES), 1).astype(F32).astype(BF16)
    row_id = lax.broadcasted_iota(jnp.int32, (ROWS, LANES), 0)
    which = lane // K
    edge_id = (lane % K) // 4 * GROUP + lane // K
    pl.semaphore_wait(barrier, peers - 1)

    def to_z(d):
        there = (my_z + d) % depth
        return pltpu.make_async_remote_copy(
            src_ref=padded, dst_ref=bank.at[me], send_sem=bank_send.at[d], recv_sem=bank_recv.at[d],
            device_id={"dom": there * 4 + me % 4}, device_id_type=MESH)

    def to_y(i):
        row = i * 4 + me % 4
        return pltpu.make_async_remote_copy(
            src_ref=bank.at[row], dst_ref=bank.at[row], send_sem=bank_send.at[depth + i],
            recv_sem=bank_recv.at[depth + i],
            device_id={"dom": my_z * 4 + (1 - my_y) * 2 + my_c}, device_id_type=MESH)

    def to_c(i):
        row = i * 2 + my_c
        return pltpu.make_async_remote_copy(
            src_ref=bank.at[row], dst_ref=bank.at[row], send_sem=bank_send.at[2 * depth + i],
            recv_sem=bank_recv.at[2 * depth + i],
            device_id={"dom": my_z * 4 + my_y * 2 + 1 - my_c}, device_id_type=MESH)

    def each(count, act, first=0):
        def step(i, carry):
            act(i)
            return carry

        lax.fori_loop(first, count, step, 0)

    own = pltpu.make_async_copy(padded, bank.at[me], local_sem.at[0])
    own.start()
    each(depth, lambda d: to_z(d).start(), 1)

    tables[1].wait()
    per = BOX // ROWS
    chunks = tiles_high // per

    def align(step, carry):
        m, b = step // (blocks // 2), step % (blocks // 2) * 2
        load(m, b).wait()
        load(m, b + 1).wait()
        sums = []

        def pixels(first, count):
            return jnp.concatenate(
                [mic[m, b + h, pl.ds(first, count)].reshape(count * ROWS, LANES) for h in range(2)], axis=1)

        def keep(n, x):
            for t in range(2):
                for h in range(2):
                    aligned[m, n, b + h, t] = x[t * ROWS : (t + 1) * ROWS, h * LANES : (h + 1) * LANES].astype(BF16)

        for a in range(chunks - 1):
            x = jnp.dot(left_t[...], pixels(a * per, 2 * per), preferred_element_type=F32)
            for n in range(PER_BOX):
                keep(a * PER_BOX + n, x[n * K : (n + 1) * K])
            sums.append(x[PER_BOX * K : PER_BOX * K + PER_BOX])
        end = pixels((chunks - 1) * per, per)
        keep((chunks - 1) * PER_BOX, jnp.dot(left_t[:K, :BOX], end, preferred_element_type=F32))
        x = jnp.dot(left_t[PER_BOX * K :, :BOX], end, preferred_element_type=F32)
        sums.append(x[:PER_BOX])
        for t in range(chunks // 2):
            pair = jnp.concatenate([sums[2 * t], sums[2 * t + 1]], axis=0).astype(BF16)
            for h in range(2):
                flat[m, t, b + h] = pair[:, h * LANES : (h + 1) * LANES]
        return carry

    lax.fori_loop(0, mics * blocks // 2, align, 0)
    for table in tables[2:]:
        table.wait()

    def peer_of(k):
        step = k // 4
        flip_z = jnp.where(step < depth // 2, depth // 2 + step, depth - 1 - step)
        return (my_z ^ flip_z) * 4 + (me + 1 + k) % 4

    def block_copy(k):
        return pltpu.make_async_remote_copy(
            src_ref=outgoing.at[k], dst_ref=arrived.at[me], send_sem=send_sem.at[k], recv_sem=recv_sem.at[k],
            device_id={"dom": peer_of(k)}, device_id_type=MESH)

    def unpack(peer, i):
        packed = info[peer, i]
        left = packed & (2**col_bits - 1)
        top = lax.shift_right_logical(packed, col_bits) & (2**row_bits - 1)
        return lax.shift_right_logical(packed, col_bits + row_bits), top, left

    def gather(k, lhs):
        for i in range(slot_cap):
            q, j = i // GROUP, i % GROUP
            m, top, left = unpack(peer_of(k), i)
            block, rl = pl.ds(lax.shift_right_logical(left, 7), 3), left & (LANES - 1)
            window = lax.shift_right_logical(top + ROWS, 5)
            tile = lax.shift_right_logical(top, 4)
            mask = lane_id >= rl.astype(F32).astype(BF16)
            coef = swap_t[top & (STEP - 1)]

            def put(t, x):
                rows = pl.ds(q * 4 * ROWS + t * ROWS, ROWS)
                lhs[rows, pl.ds(2 * j * LANES, LANES)] = jnp.where(mask, x[0], x[2])
                lhs[rows, pl.ds((2 * j + 1) * LANES, LANES)] = x[1]

            both = aligned[m, window, block]
            put(0, both[:, 0])
            put(1, both[:, 1])
            put(2, flat[m, lax.shift_right_logical(window, 4), block])
            head, tail = mic[m, block, tile], mic[m, block, tile + per]
            put(3, (tail - head) * coef)

    def finish(k, first):
        peer = peer_of(k)
        boxes = [unpack(peer, i) for i in range(slot_cap)]
        fixes = []
        for q in range(groups):
            part = first[(q * 4 + 3) * ROWS : (q * 4 + 4) * ROWS]
            odd = chain(which[:1], [(boxes[q * GROUP + j][1] >> 4) & 1 for j in range(GROUP)])
            odd = jnp.concatenate([odd, odd], axis=1) == 1
            fixes.append(jnp.concatenate([jnp.where(odd, 0.0, part), jnp.where(odd, part, 0.0)], axis=0).astype(BF16))
        fixed = jnp.dot(fix_t[...], jnp.concatenate(fixes, axis=1), preferred_element_type=F32)

        far = None
        flats = [jnp.zeros((8, LANES), F32)]
        tiles = []
        for q in range(groups):
            add = fixed[:, q * 2 * LANES : (q + 1) * 2 * LANES]
            top_rows = q * 4 * ROWS
            values, others = [], []
            for g in range(4):
                x = first[top_rows + 8 * g : top_rows + 8 * g + 8] + add[8 * g : 8 * g + 8]
                cos_part, sin_part = x[:, :LANES], flip(x[:, LANES:]) * sign
                values.append(cos_part + sin_part)
                others.append(cos_part - sin_part)
            mine = boxes[q * GROUP : (q + 1) * GROUP]
            edge = None
            for g in range(4):
                piece = pltpu.roll(others[g], g, 1) if g else others[g]
                edge = piece if edge is None else jnp.where(lane % 4 == g, piece, edge)
            edge = pltpu.roll(edge, 4 * q, 1) if q else edge
            far = edge if far is None else jnp.where(edge_id // GROUP == q, edge, far)

            at = chain(which[:1], [(lax.shift_right_logical(b[1] + ROWS, 5)) & (ROWS - 1) for b in mine])
            at = jnp.concatenate([at, at], axis=1)
            sums = first[top_rows + 2 * ROWS : top_rows + 3 * ROWS]
            rows16 = lax.broadcasted_iota(jnp.int32, (ROWS, 2 * LANES), 0)
            line = jnp.sum(jnp.where(rows16 == at, sums, 0.0), axis=0, keepdims=True) + add[K : K + 1]
            re, im = line[:, :LANES], line[:, LANES:]
            rls = [b[2] & (LANES - 1) for b in mine]
            cv = chain(which[:1], [pcol_c[pl.ds(rl, 1), :] for rl in rls])
            sv = chain(which[:1], [pcol_s[pl.ds(rl, 1), :] for rl in rls])
            weight = chain(which[:1], [ctf[b[0], 4, :1] for b in mine])
            out_re, out_im = (re * cv - im * sv) * weight, (re * sv + im * cv) * weight
            flats = [jnp.where(sub == q, out_re, jnp.where(sub == groups + q, out_im, flats[0]))]

            for j, (m, top, left) in enumerate(mine):
                total = None
                for g in range(4):
                    shift = (K * (g - j)) % LANES
                    piece = pltpu.roll(values[g], shift, 1) if shift else values[g]
                    total = piece if total is None else jnp.where(which == g, piece, total)
                rt, rl = top & (STEP - 1), left & (LANES - 1)
                cu, su = prow_c[rt], prow_s[rt]
                cv, sv = pcol_c[pl.ds(rl, 1), :], pcol_s[pl.ds(rl, 1), :]
                a = (cu * cv - su * sv) * ctf[m, 0]
                b = (su * cv + cu * sv) * ctf[m, 1]
                tiles.append(total * a + flip(total) * b)
        for i in range(slot_cap // 2):
            outgoing[k, i] = jnp.concatenate([tiles[2 * i], tiles[2 * i + 1]], axis=0).astype(BF16)

        rts = [b[1] & (STEP - 1) for b in boxes]
        ends = [b[2] & (ROWS - 1) for b in boxes]
        cu, su = chain(edge_id, [edge_c[rt] for rt in rts]), chain(edge_id, [edge_s[rt] for rt in rts])
        ce = chain(edge_id, [far_c[pl.ds(e, 1), :] for e in ends])
        se = chain(edge_id, [far_s[pl.ds(e, 1), :] for e in ends])
        weight = chain(edge_id, [ctf[b[0], 2] for b in boxes])
        far = far * (cu * ce - su * se) * weight + flip(far) * (su * ce + cu * se) * weight * sign
        low = jnp.where(sub == 2 * groups, labels[pl.ds(peer, 1), :], flats[0])
        outgoing[k, slot_cap // 2] = jnp.concatenate([far, low], axis=0).astype(BF16)

    def two_peers(i, carry):
        k = 2 * i
        first = jnp.dot(lhs_a[...], right_t[...], preferred_element_type=F32)
        gather(k + 1, lhs_b)
        finish(k, first)
        first = jnp.dot(lhs_b[...], right_t[...], preferred_element_type=F32)
        gather(jnp.minimum(k + 2, peers - 1), lhs_a)
        finish(k + 1, first)
        block_copy(k).start()

        @pl.when(k + 1 < peers - 1)
        def _():
            block_copy(k + 1).start()

        @pl.when(i == peers // 6)
        def _():
            own.wait()
            each(depth, lambda d: to_z(d).wait(), 1)
            each(depth, lambda i: to_y(i).start())

        @pl.when(i == peers // 2 - 2)
        def _():
            each(depth, lambda i: to_y(i).wait())
            each(2 * depth, lambda i: to_c(i).start())

        return carry

    info_copy.wait()
    gather(0, lhs_a)
    lax.fori_loop(0, peers // 2, two_peers, 0)
    mine = pltpu.make_async_copy(outgoing.at[peers - 1], arrived.at[me], local_sem.at[1])
    mine.start()
    each(2 * depth, lambda i: to_c(i).wait())
    each(peers - 1, lambda k: block_copy(k).wait())
    mine.wait()


def score_kernel(groups, tiles, bank_rows, pad_rows, rot_h, arrived_h, bank_h, cos_h, sin_h, edge_h, flat_h, gather_h, out_h,
                 rot, arrived, bank, cos_t, sin_t, edge_t, flat_t, gather_t, pick, spread, extras, where_v, where, out,
                 *scratch):
    halves, (sem, out_sem) = scratch[:-2], scratch[-2:]
    peers = arrived.shape[0] // tiles
    loads = [
        pltpu.make_async_copy(src, dst, sem.at[i])
        for i, (src, dst) in enumerate(
            [(rot_h, rot), (arrived_h, arrived), (edge_h, edge_t), (flat_h, flat_t), (gather_h, gather_t),
             (cos_h, cos_t), (sin_h, sin_t), (bank_h, bank)])
    ]
    for copy in loads:
        copy.start()

    loads[0].wait()
    turns, classes = rot.shape
    templates = pick.shape[1]
    turn_rows = -(-turns // 8) * 8
    named = rot[...].astype(F32)
    named = jnp.concatenate([named, jnp.zeros((turns, LANES - classes), F32)], axis=1)
    high = jnp.floor(named * (1.0 / 256))
    first = lax.broadcasted_iota(jnp.int32, (LANES, templates), 0) * turns
    spot = lax.broadcasted_iota(jnp.int32, (LANES, templates), 1) - first
    chosen = jnp.where((spot >= 0) & (spot < turns), 1.0, 0.0).astype(BF16)
    entry = 256 * jnp.dot(high.astype(BF16), chosen, preferred_element_type=F32) + jnp.dot(
        (named - 256 * high).astype(BF16), chosen, preferred_element_type=F32)
    at = lax.broadcasted_iota(jnp.int32, (turns, templates), 1).astype(F32)
    at = at - jnp.floor((at + 0.5) * (1.0 / turns)) * turns
    own = lax.broadcasted_iota(jnp.int32, (turns, templates), 0).astype(F32) == at
    entry = jnp.sum(jnp.where(own, entry, 0.0), axis=0, keepdims=True)
    entry = entry + jnp.floor((entry + 0.5) * (1.0 / bank_rows)) * (pad_rows - bank_rows)
    ids = lax.broadcasted_iota(jnp.int32, (ROWS, templates), 0)

    def mark(r, carry):
        rows = pl.ds(pl.multiple_of(r * ROWS, ROWS), ROWS)
        pick[rows, :] = jnp.where((ids + r * ROWS).astype(F32) == entry, 1.0, 0.0).astype(BF16)
        return carry

    lax.fori_loop(0, pick.shape[0] // ROWS, mark, 0)

    for copy in loads[1:4]:
        copy.wait()
    row = lax.broadcasted_iota(jnp.int32, (ROWS, LANES), 0) // GROUP

    def one(step, total):
        for i in range(8):
            p = step * 8 + i
            x = arrived[p * tiles + tiles - 1].astype(F32)
            rows = pl.ds(pl.multiple_of(p * ROWS, ROWS), ROWS)

            def line(s):
                return jnp.broadcast_to(x[s : s + 1], (ROWS, LANES))

            for s in range(8):
                spread[rows, s * LANES : (s + 1) * LANES] = line(s).astype(BF16) * edge_t[...]
            for part in range(2):
                lines = chain(row, [line(8 + part * groups + q) for q in range(groups)])
                spread[rows, (8 + part) * LANES : (9 + part) * LANES] = lines.astype(BF16) * flat_t[...]
            label = x[8 + 2 * groups : 9 + 2 * groups]
            total = total + jnp.where(label > 0.0, label + (p * ROWS - 1).astype(F32), 0.0)
        return total

    total = lax.fori_loop(0, peers // 8, one, jnp.zeros((1, LANES), F32))
    where_v[...] = jnp.broadcast_to(total, (8, LANES)).astype(jnp.int32)
    where_copy = pltpu.make_async_copy(where_v, where, sem.at[len(loads)])
    where_copy.start()
    for copy in loads[4:]:
        copy.wait()
    extras[...] = jnp.dot(spread[...], gather_t[...], preferred_element_type=F32)
    where_copy.wait()

    rows = CHUNK * SHIFTS

    def write(chunk):
        part = pl.ds(pl.multiple_of(chunk * rows, rows), rows)
        return pltpu.make_async_copy(out.at[part], out_h.at[part], out_sem.at[chunk])

    def expand(chunk, lhs):
        for n in range(CHUNK):
            slot = where[0, chunk * CHUNK + n]
            p, i = lax.shift_right_logical(slot, 4), slot & (ROWS - 1)
            pair = arrived[p * tiles + lax.shift_right_logical(i, 1)].astype(F32)
            x = jnp.where((i & 1) == 1, pair[8:], pair[:8])
            to = slice(n * SHIFTS, (n + 1) * SHIFTS)
            for k in range(4):
                re = jnp.broadcast_to(x[k : k + 1], (SHIFTS, LANES))
                im = jnp.broadcast_to(x[4 + k : 5 + k], (SHIFTS, LANES))
                c, s = cos_t[k], sin_t[k]
                lhs[to, k * LANES : (k + 1) * LANES] = (re * c - im * s).astype(BF16)
                lhs[to, (4 + k) * LANES : (5 + k) * LANES] = (re * s + im * c).astype(BF16)
            last = jnp.broadcast_to(extras[pl.ds(slot, 1), :], (8, LANES))
            turned = pltpu.roll(last, EXTRA, 1)
            last, turned = jnp.concatenate([last, last], axis=0), jnp.concatenate([turned, turned], axis=0)
            lhs[to, 8 * LANES :] = (last * cos_t[4] + turned * sin_t[4]).astype(BF16)

    def score(lhs):
        return lax.dot_general(lhs[...], bank[...], (((1,), (1,)), ((), ())),
                               preferred_element_type=F32).astype(BF16)

    def emit(chunk, scores):
        picked = jnp.dot(scores, pick[...], preferred_element_type=F32)
        out[pl.ds(pl.multiple_of(chunk * rows, rows), rows)] = picked.astype(BF16)

    def some(step, carry):
        base = step * len(halves)
        waiting = None
        for half, lhs in enumerate(halves):
            expand(base + half, lhs)
            scores = score(lhs)
            if waiting is not None:
                emit(base + half - 1, waiting)
            waiting = scores
        emit(base + len(halves) - 1, waiting)
        for half in range(len(halves)):
            write(base + half).start()
        return carry

    chunks = out.shape[0] // rows
    lax.fori_loop(0, chunks // len(halves), some, 0)
    for chunk in range(chunks):
        write(chunk).wait()


VMEM = pl.BlockSpec(memory_space=pltpu.VMEM)
HBM = pl.BlockSpec(memory_space=pltpu.HBM)
ANY = pl.BlockSpec(memory_space=pl.ANY)
SMEM = pl.BlockSpec(memory_space=pltpu.SMEM)


def body(micrographs, mic_defocus, defocus, pick_list, template_bank, rot_index):
    peers = lax.axis_size("dom")
    slot_cap = (P_DEV + peers - 1) // peers * 2
    slot_cap = -(-slot_cap // GROUP) * GROUP
    groups = slot_cap // GROUP
    mics, height, width = micrographs.shape
    row_bits, col_bits = bits(height), bits(width)
    columns = pick_list.shape[1]

    left_t, fix_t, right_t = dft_tables()
    tables = [left_t, fix_t, right_t, swap_table()] + phase_tables() + [fold_table()]
    bank_rows = template_bank.shape[0]
    pad_rows = -(-bank_rows // ROWS) * ROWS
    copies = len(tables) + mics * (width // LANES)
    tiles = slot_cap // 2 + 1
    windows = (height - BOX) // STEP + 1
    dma = pltpu.SemaphoreType.DMA
    arrived, bank = pl.pallas_call(
        functools.partial(crop_kernel, peers, slot_cap, (row_bits, col_bits)),
        out_shape=(
            jax.ShapeDtypeStruct((peers, tiles, ROWS, LANES), BF16),
            jax.ShapeDtypeStruct((peers, pad_rows, AREA), BF16),
        ),
        in_specs=[HBM] * (5 + len(tables)),
        out_specs=(ANY, ANY),
        scratch_shapes=[
            pltpu.VMEM((mics, width // LANES + 1, height // ROWS + 1, ROWS, LANES), BF16),
            *[pltpu.VMEM(t.shape, t.dtype) for t in tables],
            pltpu.SMEM((peers, LANES), jnp.int32),
            pltpu.VMEM((peers, LANES), jnp.int32),
            pltpu.SMEM(mic_defocus.shape, jnp.int32),
            pltpu.SMEM(defocus.shape, F32),
            pltpu.VMEM((4, columns), jnp.int32),
            pltpu.VMEM(template_bank.shape, BF16),
            pltpu.VMEM((peers, LANES), F32),
            pltpu.VMEM((mics, windows, width // LANES + 1, 2, ROWS, LANES), BF16),
            pltpu.VMEM((mics, height // (2 * BOX), width // LANES + 1, ROWS, LANES), BF16),
            pltpu.VMEM((mics, 6, 8, LANES), F32),
            pltpu.VMEM((groups * 4 * ROWS, GROUP * BOX), BF16),
            pltpu.VMEM((groups * 4 * ROWS, GROUP * BOX), BF16),
            pltpu.VMEM((pad_rows, AREA), BF16),
            pltpu.VMEM((peers, tiles, ROWS, LANES), BF16),
            dma((copies,)), dma((peers,)), dma((peers,)), dma((2,)), dma((peers,)), dma((peers,)), dma((5,)),
        ],
        compiler_params=pltpu.CompilerParams(
            collective_id=0, has_side_effects=True, vmem_limit_bytes=56 << 20),
        name="crop",
    )(pick_list, mic_defocus, defocus, template_bank,
      micrographs.reshape(mics, height // ROWS, ROWS, width), *[jnp.asarray(t) for t in tables])
    bank = bank.reshape(peers * pad_rows, AREA)

    templates = rot_index.size
    entries = peers * pad_rows
    rows = P_DEV * SHIFTS
    consts = shift_phases() + list(spread_tables(slot_cap))
    out = pl.pallas_call(
        functools.partial(score_kernel, groups, tiles, bank_rows, pad_rows),
        out_shape=jax.ShapeDtypeStruct((rows, templates), BF16),
        in_specs=[HBM] * (3 + len(consts)),
        out_specs=HBM,
        scratch_shapes=[
            pltpu.VMEM(rot_index.shape[::-1], jnp.int32),
            pltpu.VMEM((peers * tiles, ROWS, LANES), BF16),
            pltpu.VMEM((entries, AREA), BF16),
            *[pltpu.VMEM(c.shape, c.dtype) for c in consts],
            pltpu.VMEM((entries, templates), BF16),
            pltpu.VMEM((peers * ROWS, 10 * LANES), BF16),
            pltpu.VMEM((peers * ROWS, LANES), F32),
            pltpu.VMEM((8, LANES), jnp.int32),
            pltpu.SMEM((8, LANES), jnp.int32),
            pltpu.VMEM((rows, templates), BF16),
            *[pltpu.VMEM((CHUNK * SHIFTS, AREA), BF16)] * HALVES,
            dma((9,)),
            dma((P_DEV // CHUNK,)),
        ],
        compiler_params=pltpu.CompilerParams(vmem_limit_bytes=56 << 20),
        name="score",
    )(rot_index.T, arrived.reshape(peers * tiles, ROWS, LANES), bank, *[jnp.asarray(c) for c in consts])
    return out.reshape(P_DEV, SHIFTS, templates)


def solution(mesh):
    return jax.shard_map(
        body,
        mesh=mesh,
        in_specs=(
            P(("groups", "dom"), None, None),
            P(("groups", "dom")),
            P("groups"),
            P(None, ("groups", "dom")),
            P(("groups", "dom"), None),
            P("groups", None),
        ),
        out_specs=P(("groups", "dom"), None, None),
        check_vma=False,
    )
```

```python
import functools
import math

import jax
import jax.numpy as jnp
import ml_dtypes
import numpy as np
from jax import lax
from jax.experimental import pallas as pl
from jax.experimental.pallas import tpu as pltpu
from jax.sharding import PartitionSpec as P

BOX = 256
K = 32
HALF = K // 2
SH = 4
P_DEV = 96
SHIFTS = SH * SH
LANES = 128
ROWS = 16
STEP = 64
SWAP = STEP // 2
PER_BOX = BOX // STEP
GROUP = 4
CHUNK = 16
HALVES = 6
MAIN = K * K // 2
EXTRA = 64
AREA = 2 * (MAIN + EXTRA)

TWO_PI = 2.0 * math.pi
CHI_SCALE = 0.05
CHI_SHIFT = 0.1

MESH = pl.DeviceIdType.MESH
F32 = jnp.float32
BF16 = jnp.bfloat16


def bf(x):
    return np.asarray(x, np.float32).astype(ml_dtypes.bfloat16)


def turn(product):
    return TWO_PI * np.mod(product, BOX) / BOX


def row_order():
    return [4 * s + g - HALF for g in range(4) for s in range(4)]


def dft_tables():
    pixels = np.arange(BOX)
    scale = 1.0 / math.sqrt(BOX)
    order = np.array(row_order()).reshape(4, 4)
    cosine = np.cos(turn(order[..., None] * pixels)) * scale
    sine = -np.sin(turn(order[..., None] * pixels)) * scale
    rows = np.stack([cosine, sine], axis=1).reshape(K, BOX)
    left = np.zeros((2, PER_BOX * K + ROWS, BOX))
    for b in range(PER_BOX):
        cut = BOX - b * STEP
        left[0, b * K : (b + 1) * K, b * STEP :] = rows[:, :cut]
        left[1, b * K : (b + 1) * K, : b * STEP] = rows[:, cut:]
        left[0, PER_BOX * K + b, b * STEP :] = scale
        left[1, PER_BOX * K + b, : b * STEP] = scale
    left = np.concatenate([left[0], left[1, K:]])
    fix = np.zeros((K + ROWS, 2 * SWAP))
    fix[:K, :SWAP] = rows[:, :SWAP]
    fix[:K, SWAP:] = rows[:, -SWAP:]
    fix[K] = scale
    freq = np.arange(K) - HALF
    right = np.zeros((GROUP, BOX, 2, GROUP, K))
    for j in range(GROUP):
        right[j, :, 0, j] = np.cos(turn(freq[:, None] * pixels)).T * scale
        right[j, :, 1, j] = -np.sin(turn(freq[:, None] * pixels)).T * scale
    return bf(left), bf(fix), bf(right.reshape(GROUP * BOX, 2 * GROUP * K))


def swap_table():
    r = np.arange(ROWS)
    low = [(r < t).astype(float) for t in range(ROWS + 1)]
    high = [-(r >= t).astype(float) for t in range(ROWS + 1)]
    return bf(np.broadcast_to(np.array(low + high)[:, :, None], (2 * ROWS + 2, ROWS, LANES)))


def phase_tables():
    sub, lane = np.arange(8)[:, None], np.arange(LANES)[None, :]
    t = np.arange(STEP)[:, None, None]
    t = np.where(t < SWAP, t, t - STEP)
    rows = turn(t * (4 * (sub % 4) + lane // K - HALF))
    edge = turn(t * (4 * (sub % 4) + lane % 4 - HALF))
    cols = turn(np.arange(LANES)[:, None] * (lane % K - HALF))
    far = turn(np.arange(ROWS)[:, None] * HALF + 0 * lane)
    return [f(x).astype(np.float32) for x in (rows, edge, cols, far) for f in (np.cos, np.sin)]


def fold_table():
    table = np.zeros((MAIN, MAIN + LANES))
    for f in range(MAIN):
        u, v = f // K - HALF, f % K - HALF
        if -u < HALF and -v < HALF:
            table[-u * K + HALF - v, f] = 1
    for lane in range(K):
        table[lane, MAIN + lane] = 1
    for lane in range(1, HALF):
        table[(HALF - lane) * K, MAIN + K + lane] = 1
    return bf(table)


def shift_phases():
    moves = np.arange(SH) - SH // 2
    row_move = np.repeat(moves, SH)[:, None]
    col_move = np.tile(moves, SH)[:, None]
    f = np.arange(MAIN)
    u, v = f // K - HALF, f % K - HALF
    lane = np.arange(EXTRA)
    low = lane < K
    u = np.concatenate([u, np.where(low, 0, lane - K - HALF)])
    v = np.concatenate([v, np.where(low, lane - HALF, HALF)])
    phase = turn(row_move * u + col_move * v)
    cosine, sine = np.cos(phase), np.sin(phase)
    main = [x[:, :MAIN].reshape(SHIFTS, MAIN // LANES, LANES).transpose(1, 0, 2) for x in (cosine, sine)]
    last_c = np.concatenate([cosine[:, MAIN:]] * 2, axis=1)
    last_s = np.concatenate([-sine[:, MAIN:], sine[:, MAIN:]], axis=1)
    return [
        np.concatenate([m, x[None]]).astype(np.float32) for m, x in zip(main, (last_c, last_s), strict=True)
    ]


def spread_tables(slot_cap):
    groups = slot_cap // GROUP
    lane = np.arange(LANES)
    edge = np.zeros((ROWS, LANES))
    flat = np.zeros((ROWS, LANES))
    for i in range(slot_cap):
        q, j = i // GROUP, i % GROUP
        edge[i] = (lane // K == j) & (lane % K // 4 == q)
        flat[i] = lane // K == j
    gather = np.zeros((10, LANES, LANES))
    for s in range(8):
        gather[s, lane, EXTRA * (s // 4) + K + 4 * (s % 4) + lane % 4] = 1
    for part in range(2):
        gather[8 + part, lane, EXTRA * part + lane % K] = 1
    assert 8 + 2 * groups < ROWS and groups * 4 <= K
    return bf(edge), bf(flat), bf(gather.reshape(10 * LANES, LANES))


def bits(n):
    return (n - 1).bit_length()


def flip(x):
    return pltpu.roll(x, 4, 0)


def chain(ids, values):
    total = values[0]
    for i, value in enumerate(values[1:], 1):
        total = jnp.where(ids == i, value, total)
    return total


def crop_kernel(peers, slot_cap, shifts, pick_h, mic_def_h, defocus_h, shard_h, rot_h, mic_h, left_h, fix_h, right_h, swap_h,
                prow_ch, prow_sh, edge_ch, edge_sh, pcol_ch, pcol_sh, far_ch, far_sh, fold_h, arrived, bank, pick_out,
                mic, left_t, fix_t, right_t, swap_t, prow_c, prow_s, edge_c, edge_s, pcol_c, pcol_s, far_c, far_s, fold_t,
                info, info_v, mic_def, defocus, pick_v, shard, labels, aligned, flat, ctf, lhs_a, lhs_b, padded, outgoing, load_sem, send_sem, recv_sem, local_sem, bank_send, bank_recv, small_sem, rot, pick):
    groups = slot_cap // GROUP
    depth = peers // 4
    log_step, stack = STEP.bit_length() - 1, 3 * ROWS + SWAP
    mics, blocks, tiles_high = mic.shape[0], mic.shape[1] - 1, mic.shape[2] - SWAP // ROWS
    me = lax.axis_index("dom")
    my_z, my_y, my_c = me // 4, (me // 2) % 2, me % 2
    row_bits, col_bits = shifts

    tables = [
        pltpu.make_async_copy(src, dst, load_sem.at[i])
        for i, (src, dst) in enumerate(
            [(fold_h, fold_t), (left_h, left_t), (fix_h, fix_t), (right_h, right_t), (swap_h, swap_t),
             (prow_ch, prow_c), (prow_sh, prow_s), (edge_ch, edge_c), (edge_sh, edge_s),
             (pcol_ch, pcol_c), (pcol_sh, pcol_s), (far_ch, far_c), (far_sh, far_s)])
    ]

    def load(m, b):
        return pltpu.make_async_copy(
            mic_h.at[m, :, :, pl.ds(b * LANES, LANES)], mic.at[m, b, pl.ds(0, tiles_high)], load_sem.at[len(tables) + m * blocks + b])

    smalls = [
        pltpu.make_async_copy(src, dst, small_sem.at[i])
        for i, (src, dst) in enumerate(
            [(pick_h, pick_v), (mic_def_h, mic_def), (defocus_h, defocus), (shard_h, shard)])
    ]
    for small in smalls:
        small.start()
    tables[0].start()
    tables[1].start()
    for m in range(mics):
        for b in range(blocks):
            load(m, b).start()
    for table in tables[2:]:
        table.start()
    rot_copy = pltpu.make_async_copy(rot_h, rot, small_sem.at[5])
    rot_copy.start()

    barrier = pltpu.get_barrier_semaphore()

    def greet(k, carry):
        pl.semaphore_signal(barrier, inc=1, device_id={"dom": (me + k) % peers}, device_id_type=MESH)
        return carry

    lax.fori_loop(1, peers, greet, 0)

    smalls[0].wait()
    columns = pick_v.shape[1]
    wide = -(-columns // LANES) * LANES
    picks = pick_v[...]
    if wide > columns:
        picks = jnp.concatenate([picks, jnp.full((picks.shape[0], wide - columns), -1, jnp.int32)], axis=1)
    height, width = mic_h.shape[1] * ROWS, mic_h.shape[3]
    spot = (jnp.clip(picks[:1], 0, mics - 1) << row_bits) + jnp.clip(picks[1:2], 0, height - BOX)
    spot = (spot << col_bits) + jnp.clip(picks[2:3], 0, width - BOX)
    target = picks[3:]
    device = target * (-(-(1 << 22) // P_DEV)) >> 22
    label = target - device * P_DEV
    chosen = lax.broadcasted_iota(jnp.int32, (peers, wide), 0) == device
    pick_lane = lax.broadcasted_iota(jnp.int32, (peers, wide), 1)
    rank = chosen.astype(jnp.int32)
    for power in range((wide - 1).bit_length()):
        rank = rank + jnp.where(pick_lane >= 1 << power, pltpu.roll(rank, 1 << power, 1), 0)
    rank = jnp.where(chosen, rank, 0)
    slot_lane = lax.broadcasted_iota(jnp.int32, (peers, LANES), 1)
    spots = jnp.zeros((peers, LANES), jnp.int32)
    for i in range(slot_cap):
        here = jnp.sum(jnp.where(rank == i + 1, spot, 0), axis=1, keepdims=True)
        spots = jnp.where(slot_lane == i, here, spots)
    info_v[...] = spots
    info_copy = pltpu.make_async_copy(info_v, info, small_sem.at[4])
    info_copy.start()
    named = lax.broadcasted_iota(jnp.int32, (LANES, wide), 0) == label
    labels[...] = lax.dot_general(
        rank.astype(F32).astype(BF16), jnp.where(named, 1.0, 0.0).astype(BF16),
        (((1,), (1,)), ((), ())), preferred_element_type=F32)

    smalls[1].wait()
    smalls[2].wait()
    sub = lax.broadcasted_iota(jnp.int32, (8, LANES), 0)
    lane = lax.broadcasted_iota(jnp.int32, (8, LANES), 1)
    sign = jnp.where(sub < 4, -1.0, 1.0).astype(F32)
    lane_u = 4 * (sub % 4) - HALF
    planes = [
        (lane_u + lane // K, lane % K - HALF),
        (lane_u + lane % 4, 0 * lane + HALF),
        (0 * lane, lane % K - HALF),
    ]
    for m in range(mics):
        value = defocus[mic_def[m]]
        for i, (u, v) in enumerate(planes):
            radius = (u * u + v * v).astype(F32)
            weight = -jnp.sin(CHI_SCALE * value * radius + CHI_SHIFT)
            ctf[m, 2 * i] = weight
            ctf[m, 2 * i + 1] = weight * sign

    tables[0].wait()
    smalls[3].wait()
    half = shard.shape[1] // 4
    upper = jnp.concatenate([shard[:, half : 2 * half], shard[:, 3 * half :]], axis=0)
    folded = jnp.dot(upper, fold_t[...], preferred_element_type=F32)
    rows = shard.shape[0]
    re, im = folded[:rows], folded[rows:]
    last_lane = lax.broadcasted_iota(jnp.int32, (rows, EXTRA), 1)
    im_last = jnp.where(last_lane < K, im[:, half : half + EXTRA], -im[:, half : half + EXTRA])
    padded[...] = jnp.zeros_like(padded)
    padded[:rows] = jnp.concatenate(
        [shard[:, :half].astype(F32) + re[:, :half], shard[:, 2 * half : 3 * half].astype(F32) - im[:, :half],
         re[:, half : half + EXTRA], im_last], axis=1).astype(BF16)

    for m in range(mics):
        for b in range(blocks + 1):
            mic[m, b, tiles_high:] = jnp.zeros((SWAP // ROWS, ROWS, LANES), BF16)

    lane_id = lax.broadcasted_iota(jnp.int32, (ROWS, LANES), 1).astype(F32).astype(BF16)
    row_id = lax.broadcasted_iota(jnp.int32, (ROWS, LANES), 0)
    which = lane // K
    edge_id = (lane % K) // 4 * GROUP + lane // K
    pl.semaphore_wait(barrier, peers - 1)

    def to_z(d):
        there = (my_z + d) % depth
        return pltpu.make_async_remote_copy(
            src_ref=padded, dst_ref=bank.at[me], send_sem=bank_send.at[d], recv_sem=bank_recv.at[d],
            device_id={"dom": there * 4 + me % 4}, device_id_type=MESH)

    def to_y(i):
        row = i * 4 + me % 4
        return pltpu.make_async_remote_copy(
            src_ref=bank.at[row], dst_ref=bank.at[row], send_sem=bank_send.at[depth + i],
            recv_sem=bank_recv.at[depth + i],
            device_id={"dom": my_z * 4 + (1 - my_y) * 2 + my_c}, device_id_type=MESH)

    def to_c(i):
        row = i * 2 + my_c
        return pltpu.make_async_remote_copy(
            src_ref=bank.at[row], dst_ref=bank.at[row], send_sem=bank_send.at[2 * depth + i],
            recv_sem=bank_recv.at[2 * depth + i],
            device_id={"dom": my_z * 4 + my_y * 2 + 1 - my_c}, device_id_type=MESH)

    def each(count, act, first=0):
        def step(i, carry):
            act(i)
            return carry

        lax.fori_loop(first, count, step, 0)

    own = pltpu.make_async_copy(padded, bank.at[me], local_sem.at[0])
    own.start()
    each(depth, lambda d: to_z(d).start(), 1)

    tables[1].wait()
    per = BOX // ROWS
    chunks = tiles_high // per

    def align(step, carry):
        m, b = step // (blocks // 2), step % (blocks // 2) * 2
        load(m, b).wait()
        load(m, b + 1).wait()
        sums = []

        def pixels(first, count):
            return jnp.concatenate(
                [mic[m, b + h, pl.ds(first, count)].reshape(count * ROWS, LANES) for h in range(2)], axis=1)

        def keep(n, x):
            for t in range(2):
                for h in range(2):
                    aligned[m, n, b + h, t] = x[t * ROWS : (t + 1) * ROWS, h * LANES : (h + 1) * LANES].astype(BF16)

        size = PER_BOX * K + ROWS
        parts = [jnp.dot(left_t[...], pixels(a * per, per), preferred_element_type=F32) for a in range(chunks)]
        for a in range(chunks - 1):
            x, y = parts[a][:size], parts[a + 1][size:]
            keep(a * PER_BOX, x[:K])
            for n in range(1, PER_BOX):
                keep(a * PER_BOX + n, x[n * K : (n + 1) * K] + y[(n - 1) * K : n * K])
            sums.append(x[PER_BOX * K : PER_BOX * K + PER_BOX] + y[(PER_BOX - 1) * K : (PER_BOX - 1) * K + PER_BOX])
        keep((chunks - 1) * PER_BOX, parts[-1][:K])
        sums.append(parts[-1][PER_BOX * K : PER_BOX * K + PER_BOX])
        sums = jnp.concatenate(sums, axis=0).astype(BF16)
        for h in range(2):
            flat[m, b + h] = sums[:, h * LANES : (h + 1) * LANES]
        return carry

    lax.fori_loop(0, mics * blocks // 2, align, 0)
    for table in tables[2:]:
        table.wait()

    def peer_of(k):
        step = k // 4
        flip_z = jnp.where(step < depth // 2, depth // 2 + step, depth - 1 - step)
        return (my_z ^ flip_z) * 4 + (me + 1 + k) % 4

    def block_copy(k):
        return pltpu.make_async_remote_copy(
            src_ref=outgoing.at[k], dst_ref=arrived.at[me], send_sem=send_sem.at[k], recv_sem=recv_sem.at[k],
            device_id={"dom": peer_of(k)}, device_id_type=MESH)

    def unpack(peer, i):
        packed = info[peer, i]
        left = packed & (2**col_bits - 1)
        top = lax.shift_right_logical(packed, col_bits) & (2**row_bits - 1)
        return lax.shift_right_logical(packed, col_bits + row_bits), top, left

    def gather(k, lhs):
        for i in range(slot_cap):
            q, j = i // GROUP, i % GROUP
            m, top, left = unpack(peer_of(k), i)
            block, rl = pl.ds(lax.shift_right_logical(left, 7), 3), left & (LANES - 1)
            window = lax.shift_right_logical(top + SWAP, log_step)
            span = lax.shift_right_logical(top, log_step - 1)
            odd, cut = span & 1, top & (SWAP - 1)
            mask = lane_id >= rl.astype(F32).astype(BF16)

            def put(t, x):
                rows = pl.ds(q * stack + t * ROWS, ROWS)
                lhs[rows, pl.ds(2 * j * LANES, LANES)] = jnp.where(mask, x[0], x[2])
                lhs[rows, pl.ds((2 * j + 1) * LANES, LANES)] = x[1]

            both = aligned[m, window, block]
            put(0, both[:, 0])
            put(1, both[:, 1])
            put(2, flat[m, block])
            for t in range(SWAP // ROWS):
                tile = span * (SWAP // ROWS) + t
                head, tail = mic[m, block, tile], mic[m, block, tile + per]
                coef = swap_t[jnp.clip(cut - t * ROWS, 0, ROWS) + odd * (ROWS + 1)]
                put(3 + t, (tail - head) * coef)

    def finish(k, first):
        peer = peer_of(k)
        boxes = [unpack(peer, i) for i in range(slot_cap)]
        fixes = []
        for q in range(groups):
            part = first[q * stack + 3 * ROWS : (q + 1) * stack]
            odd = chain(which[:1], [lax.shift_right_logical(boxes[q * GROUP + j][1], log_step - 1) & 1 for j in range(GROUP)])
            odd = jnp.concatenate([odd, odd], axis=1) == 1
            fixes.append(jnp.concatenate([jnp.where(odd, 0.0, part), jnp.where(odd, part, 0.0)], axis=0).astype(BF16))
        fixed = jnp.dot(fix_t[...], jnp.concatenate(fixes, axis=1), preferred_element_type=F32)

        far = None
        flats = [jnp.zeros((8, LANES), F32)]
        tiles = []
        for q in range(groups):
            add = fixed[:, q * 2 * LANES : (q + 1) * 2 * LANES]
            top_rows = q * stack
            values, others = [], []
            for g in range(4):
                x = first[top_rows + 8 * g : top_rows + 8 * g + 8] + add[8 * g : 8 * g + 8]
                cos_part, sin_part = x[:, :LANES], flip(x[:, LANES:]) * sign
                values.append(cos_part + sin_part)
                others.append(cos_part - sin_part)
            mine = boxes[q * GROUP : (q + 1) * GROUP]
            edge = None
            for g in range(4):
                piece = pltpu.roll(others[g], g, 1) if g else others[g]
                edge = piece if edge is None else jnp.where(lane % 4 == g, piece, edge)
            edge = pltpu.roll(edge, 4 * q, 1) if q else edge
            far = edge if far is None else jnp.where(edge_id // GROUP == q, edge, far)

            at = chain(which[:1], [lax.shift_right_logical(b[1] + SWAP, log_step) for b in mine])
            at = jnp.concatenate([at, at], axis=1)
            sums = first[top_rows + 2 * ROWS : top_rows + 3 * ROWS]
            rows16 = lax.broadcasted_iota(jnp.int32, (ROWS, 2 * LANES), 0)
            line = jnp.sum(jnp.where(rows16 == at, sums, 0.0), axis=0, keepdims=True) + add[K : K + 1]
            re, im = line[:, :LANES], line[:, LANES:]
            rls = [b[2] & (LANES - 1) for b in mine]
            cv = chain(which[:1], [pcol_c[pl.ds(rl, 1), :] for rl in rls])
            sv = chain(which[:1], [pcol_s[pl.ds(rl, 1), :] for rl in rls])
            weight = chain(which[:1], [ctf[b[0], 4, :1] for b in mine])
            out_re, out_im = (re * cv - im * sv) * weight, (re * sv + im * cv) * weight
            flats = [jnp.where(sub == q, out_re, jnp.where(sub == groups + q, out_im, flats[0]))]

            for j, (m, top, left) in enumerate(mine):
                total = None
                for g in range(4):
                    shift = (K * (g - j)) % LANES
                    piece = pltpu.roll(values[g], shift, 1) if shift else values[g]
                    total = piece if total is None else jnp.where(which == g, piece, total)
                rt, rl = top & (STEP - 1), left & (LANES - 1)
                cu, su = prow_c[rt], prow_s[rt]
                cv, sv = pcol_c[pl.ds(rl, 1), :], pcol_s[pl.ds(rl, 1), :]
                a = (cu * cv - su * sv) * ctf[m, 0]
                b = (su * cv + cu * sv) * ctf[m, 1]
                tiles.append(total * a + flip(total) * b)
        for i in range(slot_cap // 2):
            outgoing[k, i] = jnp.concatenate([tiles[2 * i], tiles[2 * i + 1]], axis=0).astype(BF16)

        rts = [b[1] & (STEP - 1) for b in boxes]
        ends = [b[2] & (ROWS - 1) for b in boxes]
        cu, su = chain(edge_id, [edge_c[rt] for rt in rts]), chain(edge_id, [edge_s[rt] for rt in rts])
        ce = chain(edge_id, [far_c[pl.ds(e, 1), :] for e in ends])
        se = chain(edge_id, [far_s[pl.ds(e, 1), :] for e in ends])
        weight = chain(edge_id, [ctf[b[0], 2] for b in boxes])
        far = far * (cu * ce - su * se) * weight + flip(far) * (su * ce + cu * se) * weight * sign
        low = jnp.where(sub == 2 * groups, labels[pl.ds(peer, 1), :], flats[0])
        outgoing[k, slot_cap // 2] = jnp.concatenate([far, low], axis=0).astype(BF16)

    def two_peers(i, carry):
        k = 2 * i
        first = jnp.dot(lhs_a[...], right_t[...], preferred_element_type=F32)
        gather(k + 1, lhs_b)
        finish(k, first)
        first = jnp.dot(lhs_b[...], right_t[...], preferred_element_type=F32)
        gather(jnp.minimum(k + 2, peers - 1), lhs_a)
        finish(k + 1, first)
        block_copy(k).start()

        @pl.when(k + 1 < peers - 1)
        def _():
            block_copy(k + 1).start()

        @pl.when(i == peers // 6)
        def _():
            own.wait()
            each(depth, lambda d: to_z(d).wait(), 1)
            each(depth, lambda i: to_y(i).start())

        @pl.when(i == peers // 2 - 2)
        def _():
            each(depth, lambda i: to_y(i).wait())
            each(2 * depth, lambda i: to_c(i).start())

        return carry

    info_copy.wait()
    gather(0, lhs_a)
    lax.fori_loop(0, peers // 2, two_peers, 0)
    mine = pltpu.make_async_copy(outgoing.at[peers - 1], arrived.at[me], local_sem.at[1])
    mine.start()

    rot_copy.wait()
    turns, classes = rot.shape
    templates = pick.shape[1]
    named = rot[...].astype(F32)
    named = jnp.concatenate([named, jnp.zeros((turns, LANES - classes), F32)], axis=1)
    high = jnp.floor(named * (1.0 / 256))
    start = lax.broadcasted_iota(jnp.int32, (LANES, templates), 0) * turns
    spot = lax.broadcasted_iota(jnp.int32, (LANES, templates), 1) - start
    chosen = jnp.where((spot >= 0) & (spot < turns), 1.0, 0.0).astype(BF16)
    entry = 256 * jnp.dot(high.astype(BF16), chosen, preferred_element_type=F32) + jnp.dot(
        (named - 256 * high).astype(BF16), chosen, preferred_element_type=F32)
    at = lax.broadcasted_iota(jnp.int32, (turns, templates), 1).astype(F32)
    at = at - jnp.floor((at + 0.5) * (1.0 / turns)) * turns
    own = lax.broadcasted_iota(jnp.int32, (turns, templates), 0).astype(F32) == at
    entry = jnp.sum(jnp.where(own, entry, 0.0), axis=0, keepdims=True)
    entry = entry + jnp.floor((entry + 0.5) * (1.0 / shard.shape[0])) * (padded.shape[0] - shard.shape[0])
    ids = lax.broadcasted_iota(jnp.int32, (ROWS, templates), 0)

    def mark(r, carry):
        rows = pl.ds(pl.multiple_of(r * ROWS, ROWS), ROWS)
        pick[rows, :] = jnp.where((ids + r * ROWS).astype(F32) == entry, 1.0, 0.0).astype(BF16)
        return carry

    lax.fori_loop(0, pick.shape[0] // ROWS, mark, 0)
    pick_copy = pltpu.make_async_copy(pick, pick_out, small_sem.at[6])
    pick_copy.start()

    each(2 * depth, lambda i: to_c(i).wait())
    each(peers - 1, lambda k: block_copy(k).wait())
    mine.wait()
    pick_copy.wait()


def score_kernel(groups, tiles, arrived_h, bank_h, pick_h, cos_h, sin_h, edge_h, flat_h, gather_h, out_h,
                 arrived, bank, cos_t, sin_t, edge_t, flat_t, gather_t, pick, spread, extras, where_v, where, out,
                 *scratch):
    halves, (sem, out_sem) = scratch[:-2], scratch[-2:]
    peers = arrived.shape[0] // tiles
    loads = [
        pltpu.make_async_copy(src, dst, sem.at[i])
        for i, (src, dst) in enumerate(
            [(arrived_h, arrived), (edge_h, edge_t), (flat_h, flat_t), (gather_h, gather_t),
             (cos_h, cos_t), (sin_h, sin_t), (bank_h, bank), (pick_h, pick)])
    ]
    for copy in loads:
        copy.start()

    for copy in loads[:3]:
        copy.wait()
    row = lax.broadcasted_iota(jnp.int32, (ROWS, LANES), 0) // GROUP

    def one(step, total):
        for i in range(8):
            p = step * 8 + i
            x = arrived[p * tiles + tiles - 1].astype(F32)
            rows = pl.ds(pl.multiple_of(p * ROWS, ROWS), ROWS)

            def line(s):
                return jnp.broadcast_to(x[s : s + 1], (ROWS, LANES))

            for s in range(8):
                spread[rows, s * LANES : (s + 1) * LANES] = line(s).astype(BF16) * edge_t[...]
            for part in range(2):
                lines = chain(row, [line(8 + part * groups + q) for q in range(groups)])
                spread[rows, (8 + part) * LANES : (9 + part) * LANES] = lines.astype(BF16) * flat_t[...]
            label = x[8 + 2 * groups : 9 + 2 * groups]
            total = total + jnp.where(label > 0.0, label + (p * ROWS - 1).astype(F32), 0.0)
        return total

    total = lax.fori_loop(0, peers // 8, one, jnp.zeros((1, LANES), F32))
    where_v[...] = jnp.broadcast_to(total, (8, LANES)).astype(jnp.int32)
    where_copy = pltpu.make_async_copy(where_v, where, sem.at[len(loads)])
    where_copy.start()
    loads[3].wait()
    extras[...] = jnp.dot(spread[...], gather_t[...], preferred_element_type=F32)
    where_copy.wait()
    for copy in loads[4:]:
        copy.wait()

    rows = CHUNK * SHIFTS

    def write(chunk):
        part = pl.ds(pl.multiple_of(chunk * rows, rows), rows)
        return pltpu.make_async_copy(out.at[part], out_h.at[part], out_sem.at[chunk])

    def expand(chunk, lhs):
        for n in range(CHUNK):
            slot = where[0, chunk * CHUNK + n]
            p, i = lax.shift_right_logical(slot, 4), slot & (ROWS - 1)
            pair = arrived[p * tiles + lax.shift_right_logical(i, 1)].astype(F32)
            x = jnp.where((i & 1) == 1, pair[8:], pair[:8])
            to = slice(n * SHIFTS, (n + 1) * SHIFTS)
            for k in range(4):
                re = jnp.broadcast_to(x[k : k + 1], (SHIFTS, LANES))
                im = jnp.broadcast_to(x[4 + k : 5 + k], (SHIFTS, LANES))
                c, s = cos_t[k], sin_t[k]
                lhs[to, k * LANES : (k + 1) * LANES] = (re * c - im * s).astype(BF16)
                lhs[to, (4 + k) * LANES : (5 + k) * LANES] = (re * s + im * c).astype(BF16)
            last = jnp.broadcast_to(extras[pl.ds(slot, 1), :], (8, LANES))
            turned = pltpu.roll(last, EXTRA, 1)
            last, turned = jnp.concatenate([last, last], axis=0), jnp.concatenate([turned, turned], axis=0)
            lhs[to, 8 * LANES :] = (last * cos_t[4] + turned * sin_t[4]).astype(BF16)

    def score(lhs):
        return lax.dot_general(lhs[...], bank[...], (((1,), (1,)), ((), ())),
                               preferred_element_type=F32).astype(BF16)

    def emit(chunk, scores):
        picked = jnp.dot(scores, pick[...], preferred_element_type=F32)
        out[pl.ds(pl.multiple_of(chunk * rows, rows), rows)] = picked.astype(BF16)

    def some(step, carry):
        base = step * len(halves)
        waiting = None
        for half, lhs in enumerate(halves):
            expand(base + half, lhs)
            scores = score(lhs)
            if waiting is not None:
                emit(base + half - 1, waiting)
                write(base + half - 1).start()
            waiting = scores
        emit(base + len(halves) - 1, waiting)
        write(base + len(halves) - 1).start()
        return carry

    chunks = out.shape[0] // rows
    lax.fori_loop(0, chunks // len(halves), some, 0)
    for chunk in range(chunks):
        write(chunk).wait()


VMEM = pl.BlockSpec(memory_space=pltpu.VMEM)
HBM = pl.BlockSpec(memory_space=pltpu.HBM)
ANY = pl.BlockSpec(memory_space=pl.ANY)
SMEM = pl.BlockSpec(memory_space=pltpu.SMEM)


def body(micrographs, mic_defocus, defocus, pick_list, template_bank, rot_index):
    peers = lax.axis_size("dom")
    slot_cap = (P_DEV + peers - 1) // peers * 2
    slot_cap = -(-slot_cap // GROUP) * GROUP
    groups = slot_cap // GROUP
    mics, height, width = micrographs.shape
    row_bits, col_bits = bits(height), bits(width)
    columns = pick_list.shape[1]

    left_t, fix_t, right_t = dft_tables()
    tables = [left_t, fix_t, right_t, swap_table()] + phase_tables() + [fold_table()]
    bank_rows = template_bank.shape[0]
    pad_rows = -(-bank_rows // ROWS) * ROWS
    copies = len(tables) + mics * (width // LANES)
    tiles = slot_cap // 2 + 1
    windows = (height - BOX) // STEP + 1
    dma = pltpu.SemaphoreType.DMA
    templates = rot_index.size
    entries = peers * pad_rows
    arrived, bank, pick = pl.pallas_call(
        functools.partial(crop_kernel, peers, slot_cap, (row_bits, col_bits)),
        out_shape=(
            jax.ShapeDtypeStruct((peers, tiles, ROWS, LANES), BF16),
            jax.ShapeDtypeStruct((peers, pad_rows, AREA), BF16),
            jax.ShapeDtypeStruct((entries, templates), BF16),
        ),
        in_specs=[HBM] * (6 + len(tables)),
        out_specs=(ANY, ANY, ANY),
        scratch_shapes=[
            pltpu.VMEM((mics, width // LANES + 1, (height + SWAP) // ROWS, ROWS, LANES), BF16),
            *[pltpu.VMEM(t.shape, t.dtype) for t in tables],
            pltpu.SMEM((peers, LANES), jnp.int32),
            pltpu.VMEM((peers, LANES), jnp.int32),
            pltpu.SMEM(mic_defocus.shape, jnp.int32),
            pltpu.SMEM(defocus.shape, F32),
            pltpu.VMEM((4, columns), jnp.int32),
            pltpu.VMEM(template_bank.shape, BF16),
            pltpu.VMEM((peers, LANES), F32),
            pltpu.VMEM((mics, windows, width // LANES + 1, 2, ROWS, LANES), BF16),
            pltpu.VMEM((mics, width // LANES + 1, ROWS, LANES), BF16),
            pltpu.VMEM((mics, 6, 8, LANES), F32),
            pltpu.VMEM((groups * (3 * ROWS + SWAP), GROUP * BOX), BF16),
            pltpu.VMEM((groups * (3 * ROWS + SWAP), GROUP * BOX), BF16),
            pltpu.VMEM((pad_rows, AREA), BF16),
            pltpu.VMEM((peers, tiles, ROWS, LANES), BF16),
            dma((copies,)), dma((peers,)), dma((peers,)), dma((2,)), dma((peers,)), dma((peers,)), dma((7,)),
            pltpu.VMEM(rot_index.shape[::-1], jnp.int32),
            pltpu.VMEM((entries, templates), BF16),
        ],
        compiler_params=pltpu.CompilerParams(
            collective_id=0, has_side_effects=True, vmem_limit_bytes=56 << 20),
        name="crop",
    )(pick_list, mic_defocus, defocus, template_bank, rot_index.T,
      micrographs.reshape(mics, height // ROWS, ROWS, width), *[jnp.asarray(t) for t in tables])
    bank = bank.reshape(peers * pad_rows, AREA)

    rows = P_DEV * SHIFTS
    consts = shift_phases() + list(spread_tables(slot_cap))
    out = pl.pallas_call(
        functools.partial(score_kernel, groups, tiles),
        out_shape=jax.ShapeDtypeStruct((rows, templates), BF16),
        in_specs=[HBM] * (3 + len(consts)),
        out_specs=HBM,
        scratch_shapes=[
            pltpu.VMEM((peers * tiles, ROWS, LANES), BF16),
            pltpu.VMEM((entries, AREA), BF16),
            *[pltpu.VMEM(c.shape, c.dtype) for c in consts],
            pltpu.VMEM((entries, templates), BF16),
            pltpu.VMEM((peers * ROWS, 10 * LANES), BF16),
            pltpu.VMEM((peers * ROWS, LANES), F32),
            pltpu.VMEM((8, LANES), jnp.int32),
            pltpu.SMEM((8, LANES), jnp.int32),
            pltpu.VMEM((rows, templates), BF16),
            *[pltpu.VMEM((CHUNK * SHIFTS, AREA), BF16)] * HALVES,
            dma((9,)),
            dma((P_DEV // CHUNK,)),
        ],
        compiler_params=pltpu.CompilerParams(vmem_limit_bytes=56 << 20),
        name="score",
    )(arrived.reshape(peers * tiles, ROWS, LANES), bank, pick, *[jnp.asarray(c) for c in consts])
    return out.reshape(P_DEV, SHIFTS, templates)


def solution(mesh):
    return jax.shard_map(
        body,
        mesh=mesh,
        in_specs=(
            P(("groups", "dom"), None, None),
            P(("groups", "dom")),
            P("groups"),
            P(None, ("groups", "dom")),
            P(("groups", "dom"), None),
            P("groups", None),
        ),
        out_specs=P(("groups", "dom"), None, None),
        check_vma=False,
    )
```

```python
import functools
import math

import jax
import jax.numpy as jnp
import ml_dtypes
import numpy as np
from jax import lax
from jax.experimental import pallas as pl
from jax.experimental.pallas import tpu as pltpu
from jax.sharding import PartitionSpec as P

BOX = 256
K = 32
HALF = K // 2
SH = 4
P_DEV = 96
SHIFTS = SH * SH
LANES = 128
ROWS = 16
STEP = 64
SWAP = STEP // 2
PER_BOX = BOX // STEP
GROUP = 4
CHUNK = 16
HALVES = 6
MAIN = K * K // 2
EXTRA = 64
AREA = 2 * (MAIN + EXTRA)

TWO_PI = 2.0 * math.pi
CHI_SCALE = 0.05
CHI_SHIFT = 0.1

MESH = pl.DeviceIdType.MESH
F32 = jnp.float32
BF16 = jnp.bfloat16


def bf(x):
    return np.asarray(x, np.float32).astype(ml_dtypes.bfloat16)


def turn(product):
    return TWO_PI * np.mod(product, BOX) / BOX


def row_order():
    return [4 * s + g - HALF for g in range(4) for s in range(4)]


def dft_tables():
    pixels = np.arange(BOX)
    scale = 1.0 / math.sqrt(BOX)
    order = np.array(row_order()).reshape(4, 4)
    cosine = np.cos(turn(order[..., None] * pixels)) * scale
    sine = -np.sin(turn(order[..., None] * pixels)) * scale
    rows = np.stack([cosine, sine], axis=1).reshape(K, BOX)
    left = np.zeros((2, PER_BOX * K + ROWS, BOX))
    for b in range(PER_BOX):
        cut = BOX - b * STEP
        left[0, b * K : (b + 1) * K, b * STEP :] = rows[:, :cut]
        left[1, b * K : (b + 1) * K, : b * STEP] = rows[:, cut:]
        left[0, PER_BOX * K + b, b * STEP :] = scale
        left[1, PER_BOX * K + b, : b * STEP] = scale
    left = np.concatenate([left[0], left[1, K:]])
    fix = np.zeros((K + ROWS, 2 * SWAP))
    fix[:K, :SWAP] = rows[:, :SWAP]
    fix[:K, SWAP:] = rows[:, -SWAP:]
    fix[K] = scale
    freq = np.arange(K) - HALF
    right = np.zeros((GROUP, BOX, 2, GROUP, K))
    for j in range(GROUP):
        right[j, :, 0, j] = np.cos(turn(freq[:, None] * pixels)).T * scale
        right[j, :, 1, j] = -np.sin(turn(freq[:, None] * pixels)).T * scale
    return bf(left), bf(fix), bf(right.reshape(GROUP * BOX, 2 * GROUP * K))


def swap_table():
    r = np.arange(ROWS)
    low = [(r < t).astype(float) for t in range(ROWS + 1)]
    high = [-(r >= t).astype(float) for t in range(ROWS + 1)]
    return bf(np.broadcast_to(np.array(low + high)[:, :, None], (2 * ROWS + 2, ROWS, LANES)))


def phase_tables():
    sub, lane = np.arange(8)[:, None], np.arange(LANES)[None, :]
    t = np.arange(STEP)[:, None, None]
    t = np.where(t < SWAP, t, t - STEP)
    rows = turn(t * (4 * (sub % 4) + lane // K - HALF))
    edge = turn(t * (4 * (sub % 4) + lane % 4 - HALF))
    cols = turn(np.arange(LANES)[:, None] * (lane % K - HALF))
    far = turn(np.arange(ROWS)[:, None] * HALF + 0 * lane)
    return [f(x).astype(np.float32) for x in (rows, edge, cols, far) for f in (np.cos, np.sin)]


def fold_table():
    table = np.zeros((MAIN, MAIN + LANES))
    for f in range(MAIN):
        u, v = f // K - HALF, f % K - HALF
        if -u < HALF and -v < HALF:
            table[-u * K + HALF - v, f] = 1
    for lane in range(K):
        table[lane, MAIN + lane] = 1
    for lane in range(1, HALF):
        table[(HALF - lane) * K, MAIN + K + lane] = 1
    return bf(table)


def shift_phases():
    moves = np.arange(SH) - SH // 2
    row_move = np.repeat(moves, SH)[:, None]
    col_move = np.tile(moves, SH)[:, None]
    f = np.arange(MAIN)
    u, v = f // K - HALF, f % K - HALF
    lane = np.arange(EXTRA)
    low = lane < K
    u = np.concatenate([u, np.where(low, 0, lane - K - HALF)])
    v = np.concatenate([v, np.where(low, lane - HALF, HALF)])
    phase = turn(row_move * u + col_move * v)
    cosine, sine = np.cos(phase), np.sin(phase)
    main = [x[:, :MAIN].reshape(SHIFTS, MAIN // LANES, LANES).transpose(1, 0, 2) for x in (cosine, sine)]
    last_c = np.concatenate([cosine[:, MAIN:]] * 2, axis=1)
    last_s = np.concatenate([-sine[:, MAIN:], sine[:, MAIN:]], axis=1)
    return [
        np.concatenate([m, x[None]]).astype(np.float32) for m, x in zip(main, (last_c, last_s), strict=True)
    ]


def spread_tables(slot_cap):
    groups = slot_cap // GROUP
    lane = np.arange(LANES)
    edge = np.zeros((ROWS, LANES))
    flat = np.zeros((ROWS, LANES))
    for i in range(slot_cap):
        q, j = i // GROUP, i % GROUP
        edge[i] = (lane // K == j) & (lane % K // 4 == q)
        flat[i] = lane // K == j
    gather = np.zeros((10, LANES, LANES))
    for s in range(8):
        gather[s, lane, EXTRA * (s // 4) + K + 4 * (s % 4) + lane % 4] = 1
    for part in range(2):
        gather[8 + part, lane, EXTRA * part + lane % K] = 1
    assert 8 + 2 * groups < ROWS and groups * 4 <= K
    return bf(edge), bf(flat), bf(gather.reshape(10 * LANES, LANES))


def bits(n):
    return (n - 1).bit_length()


def flip(x):
    return pltpu.roll(x, 4, 0)


def chain(ids, values):
    total = values[0]
    for i, value in enumerate(values[1:], 1):
        total = jnp.where(ids == i, value, total)
    return total


def crop_kernel(peers, slot_cap, shifts, pick_h, mic_def_h, defocus_h, shard_h, rot_h, mic_h, left_h, fix_h, right_h, swap_h,
                prow_ch, prow_sh, edge_ch, edge_sh, pcol_ch, pcol_sh, far_ch, far_sh, fold_h, arrived, bank, pick_out,
                mic, left_t, fix_t, right_t, swap_t, prow_c, prow_s, edge_c, edge_s, pcol_c, pcol_s, far_c, far_s, fold_t,
                info, info_v, mic_def, defocus, pick_v, shard, labels, aligned, flat, ctf, lhs_a, lhs_b, padded, outgoing, load_sem, send_sem, recv_sem, local_sem, bank_send, bank_recv, small_sem, rot, pick):
    groups = slot_cap // GROUP
    depth = peers // 4
    log_step, stack = STEP.bit_length() - 1, 3 * ROWS + SWAP
    mics, blocks, tiles_high = mic.shape[0], mic.shape[1] - 1, mic.shape[2] - SWAP // ROWS
    me = lax.axis_index("dom")
    my_z, my_y, my_c = me // 4, (me // 2) % 2, me % 2
    row_bits, col_bits = shifts

    tables = [
        pltpu.make_async_copy(src, dst, load_sem.at[i])
        for i, (src, dst) in enumerate(
            [(fold_h, fold_t), (left_h, left_t), (fix_h, fix_t), (right_h, right_t), (swap_h, swap_t),
             (prow_ch, prow_c), (prow_sh, prow_s), (edge_ch, edge_c), (edge_sh, edge_s),
             (pcol_ch, pcol_c), (pcol_sh, pcol_s), (far_ch, far_c), (far_sh, far_s)])
    ]

    def load(m, b):
        return pltpu.make_async_copy(
            mic_h.at[m, :, :, pl.ds(b * LANES, LANES)], mic.at[m, b, pl.ds(0, tiles_high)], load_sem.at[len(tables) + m * blocks + b])

    smalls = [
        pltpu.make_async_copy(src, dst, small_sem.at[i])
        for i, (src, dst) in enumerate(
            [(pick_h, pick_v), (mic_def_h, mic_def), (defocus_h, defocus), (shard_h, shard)])
    ]
    for small in smalls:
        small.start()
    tables[0].start()
    tables[1].start()
    for m in range(mics):
        for b in range(blocks):
            load(m, b).start()
    for table in tables[2:]:
        table.start()
    rot_copy = pltpu.make_async_copy(rot_h, rot, small_sem.at[5])
    rot_copy.start()

    barrier = pltpu.get_barrier_semaphore()

    def greet(k, carry):
        pl.semaphore_signal(barrier, inc=1, device_id={"dom": (me + k) % peers}, device_id_type=MESH)
        return carry

    lax.fori_loop(1, peers, greet, 0)

    smalls[0].wait()
    columns = pick_v.shape[1]
    wide = -(-columns // LANES) * LANES
    picks = pick_v[...]
    if wide > columns:
        picks = jnp.concatenate([picks, jnp.full((picks.shape[0], wide - columns), -1, jnp.int32)], axis=1)
    height, width = mic_h.shape[1] * ROWS, mic_h.shape[3]
    spot = (jnp.clip(picks[:1], 0, mics - 1) << row_bits) + jnp.clip(picks[1:2], 0, height - BOX)
    spot = (spot << col_bits) + jnp.clip(picks[2:3], 0, width - BOX)
    target = picks[3:]
    device = target * (-(-(1 << 22) // P_DEV)) >> 22
    label = target - device * P_DEV
    chosen = lax.broadcasted_iota(jnp.int32, (peers, wide), 0) == device
    pick_lane = lax.broadcasted_iota(jnp.int32, (peers, wide), 1)
    rank = chosen.astype(jnp.int32)
    for power in range((wide - 1).bit_length()):
        rank = rank + jnp.where(pick_lane >= 1 << power, pltpu.roll(rank, 1 << power, 1), 0)
    rank = jnp.where(chosen, rank, 0)
    slot_lane = lax.broadcasted_iota(jnp.int32, (peers, LANES), 1)
    spots = jnp.zeros((peers, LANES), jnp.int32)
    for i in range(slot_cap):
        here = jnp.sum(jnp.where(rank == i + 1, spot, 0), axis=1, keepdims=True)
        spots = jnp.where(slot_lane == i, here, spots)
    info_v[...] = spots
    info_copy = pltpu.make_async_copy(info_v, info, small_sem.at[4])
    info_copy.start()
    named = lax.broadcasted_iota(jnp.int32, (LANES, wide), 0) == label
    labels[...] = lax.dot_general(
        rank.astype(F32).astype(BF16), jnp.where(named, 1.0, 0.0).astype(BF16),
        (((1,), (1,)), ((), ())), preferred_element_type=F32)

    smalls[1].wait()
    smalls[2].wait()
    sub = lax.broadcasted_iota(jnp.int32, (8, LANES), 0)
    lane = lax.broadcasted_iota(jnp.int32, (8, LANES), 1)
    sign = jnp.where(sub < 4, -1.0, 1.0).astype(F32)
    lane_u = 4 * (sub % 4) - HALF
    planes = [
        (lane_u + lane // K, lane % K - HALF),
        (lane_u + lane % 4, 0 * lane + HALF),
        (0 * lane, lane % K - HALF),
    ]
    for m in range(mics):
        value = defocus[mic_def[m]]
        for i, (u, v) in enumerate(planes):
            radius = (u * u + v * v).astype(F32)
            weight = -jnp.sin(CHI_SCALE * value * radius + CHI_SHIFT)
            ctf[m, 2 * i] = weight
            ctf[m, 2 * i + 1] = weight * sign

    tables[0].wait()
    smalls[3].wait()
    half = shard.shape[1] // 4
    upper = jnp.concatenate([shard[:, half : 2 * half], shard[:, 3 * half :]], axis=0)
    folded = jnp.dot(upper, fold_t[...], preferred_element_type=F32)
    rows = shard.shape[0]
    re, im = folded[:rows], folded[rows:]
    last_lane = lax.broadcasted_iota(jnp.int32, (rows, EXTRA), 1)
    im_last = jnp.where(last_lane < K, im[:, half : half + EXTRA], -im[:, half : half + EXTRA])
    padded[...] = jnp.zeros_like(padded)
    padded[:rows] = jnp.concatenate(
        [shard[:, :half].astype(F32) + re[:, :half], shard[:, 2 * half : 3 * half].astype(F32) - im[:, :half],
         re[:, half : half + EXTRA], im_last], axis=1).astype(BF16)

    for m in range(mics):
        for b in range(blocks + 1):
            mic[m, b, tiles_high:] = jnp.zeros((SWAP // ROWS, ROWS, LANES), BF16)

    lane_id = lax.broadcasted_iota(jnp.int32, (ROWS, LANES), 1).astype(F32).astype(BF16)
    row_id = lax.broadcasted_iota(jnp.int32, (ROWS, LANES), 0)
    which = lane // K
    edge_id = (lane % K) // 4 * GROUP + lane // K
    pl.semaphore_wait(barrier, peers - 1)

    def to_z(d):
        there = (my_z + d) % depth
        return pltpu.make_async_remote_copy(
            src_ref=padded, dst_ref=bank.at[me], send_sem=bank_send.at[d], recv_sem=bank_recv.at[d],
            device_id={"dom": there * 4 + me % 4}, device_id_type=MESH)

    def to_y(i):
        row = i * 4 + me % 4
        return pltpu.make_async_remote_copy(
            src_ref=bank.at[row], dst_ref=bank.at[row], send_sem=bank_send.at[depth + i],
            recv_sem=bank_recv.at[depth + i],
            device_id={"dom": my_z * 4 + (1 - my_y) * 2 + my_c}, device_id_type=MESH)

    def to_c(i):
        row = i * 2 + my_c
        return pltpu.make_async_remote_copy(
            src_ref=bank.at[row], dst_ref=bank.at[row], send_sem=bank_send.at[2 * depth + i],
            recv_sem=bank_recv.at[2 * depth + i],
            device_id={"dom": my_z * 4 + my_y * 2 + 1 - my_c}, device_id_type=MESH)

    def each(count, act, first=0):
        def step(i, carry):
            act(i)
            return carry

        lax.fori_loop(first, count, step, 0)

    own = pltpu.make_async_copy(padded, bank.at[me], local_sem.at[0])
    own.start()
    each(depth, lambda d: to_z(d).start(), 1)

    tables[1].wait()
    per = BOX // ROWS
    chunks = tiles_high // per

    def align(step):
        m, b = step // (blocks // 2), step % (blocks // 2) * 2
        sums = []

        def pixels(first, count):
            return jnp.concatenate(
                [mic[m, b + h, pl.ds(first, count)].reshape(count * ROWS, LANES) for h in range(2)], axis=1)

        def keep(n, x):
            for t in range(2):
                for h in range(2):
                    aligned[m, n, b + h, t] = x[t * ROWS : (t + 1) * ROWS, h * LANES : (h + 1) * LANES].astype(BF16)

        size = PER_BOX * K + ROWS
        parts = [jnp.dot(left_t[...], pixels(a * per, per), preferred_element_type=F32) for a in range(chunks)]
        for a in range(chunks - 1):
            x, y = parts[a][:size], parts[a + 1][size:]
            keep(a * PER_BOX, x[:K])
            for n in range(1, PER_BOX):
                keep(a * PER_BOX + n, x[n * K : (n + 1) * K] + y[(n - 1) * K : n * K])
            sums.append(x[PER_BOX * K : PER_BOX * K + PER_BOX] + y[(PER_BOX - 1) * K : (PER_BOX - 1) * K + PER_BOX])
        keep((chunks - 1) * PER_BOX, parts[-1][:K])
        sums.append(parts[-1][PER_BOX * K : PER_BOX * K + PER_BOX])
        sums = jnp.concatenate(sums, axis=0).astype(BF16)
        for h in range(2):
            flat[m, b + h] = sums[:, h * LANES : (h + 1) * LANES]

    def two_steps(i, carry):
        for n in range(4):
            load((4 * i + n) // blocks, (4 * i + n) % blocks).wait()
        align(2 * i)
        align(2 * i + 1)
        return carry

    lax.fori_loop(0, mics * blocks // 4, two_steps, 0)
    for table in tables[2:]:
        table.wait()

    def peer_of(k):
        step = k // 4
        flip_z = jnp.where(step < depth // 2, depth // 2 + step, depth - 1 - step)
        return (my_z ^ flip_z) * 4 + (me + 1 + k) % 4

    def block_copy(k):
        return pltpu.make_async_remote_copy(
            src_ref=outgoing.at[k], dst_ref=arrived.at[me], send_sem=send_sem.at[k], recv_sem=recv_sem.at[k],
            device_id={"dom": peer_of(k)}, device_id_type=MESH)

    def unpack(peer, i):
        packed = info[peer, i]
        left = packed & (2**col_bits - 1)
        top = lax.shift_right_logical(packed, col_bits) & (2**row_bits - 1)
        return lax.shift_right_logical(packed, col_bits + row_bits), top, left

    def gather(k, lhs):
        for i in range(slot_cap):
            q, j = i // GROUP, i % GROUP
            m, top, left = unpack(peer_of(k), i)
            block, rl = pl.ds(lax.shift_right_logical(left, 7), 3), left & (LANES - 1)
            window = lax.shift_right_logical(top + SWAP, log_step)
            span = lax.shift_right_logical(top, log_step - 1)
            odd, cut = span & 1, top & (SWAP - 1)
            mask = lane_id >= rl.astype(F32).astype(BF16)

            def put(t, x):
                rows = pl.ds(q * stack + t * ROWS, ROWS)
                lhs[rows, pl.ds(2 * j * LANES, LANES)] = jnp.where(mask, x[0], x[2])
                lhs[rows, pl.ds((2 * j + 1) * LANES, LANES)] = x[1]

            both = aligned[m, window, block]
            put(0, both[:, 0])
            put(1, both[:, 1])
            put(2, flat[m, block])
            for t in range(SWAP // ROWS):
                tile = span * (SWAP // ROWS) + t
                head, tail = mic[m, block, tile], mic[m, block, tile + per]
                coef = swap_t[jnp.clip(cut - t * ROWS, 0, ROWS) + odd * (ROWS + 1)]
                put(3 + t, (tail - head) * coef)

    def finish(k, first):
        peer = peer_of(k)
        boxes = [unpack(peer, i) for i in range(slot_cap)]
        fixes = []
        for q in range(groups):
            part = first[q * stack + 3 * ROWS : (q + 1) * stack]
            odd = chain(which[:1], [lax.shift_right_logical(boxes[q * GROUP + j][1], log_step - 1) & 1 for j in range(GROUP)])
            odd = jnp.concatenate([odd, odd], axis=1) == 1
            fixes.append(jnp.concatenate([jnp.where(odd, 0.0, part), jnp.where(odd, part, 0.0)], axis=0).astype(BF16))
        fixed = jnp.dot(fix_t[...], jnp.concatenate(fixes, axis=1), preferred_element_type=F32)

        far = None
        flats = [jnp.zeros((8, LANES), F32)]
        tiles = []
        for q in range(groups):
            add = fixed[:, q * 2 * LANES : (q + 1) * 2 * LANES]
            top_rows = q * stack
            values, others = [], []
            for g in range(4):
                x = first[top_rows + 8 * g : top_rows + 8 * g + 8] + add[8 * g : 8 * g + 8]
                cos_part, sin_part = x[:, :LANES], flip(x[:, LANES:]) * sign
                values.append(cos_part + sin_part)
                others.append(cos_part - sin_part)
            mine = boxes[q * GROUP : (q + 1) * GROUP]
            edge = None
            for g in range(4):
                piece = pltpu.roll(others[g], g, 1) if g else others[g]
                edge = piece if edge is None else jnp.where(lane % 4 == g, piece, edge)
            edge = pltpu.roll(edge, 4 * q, 1) if q else edge
            far = edge if far is None else jnp.where(edge_id // GROUP == q, edge, far)

            at = chain(which[:1], [lax.shift_right_logical(b[1] + SWAP, log_step) for b in mine])
            at = jnp.concatenate([at, at], axis=1)
            sums = first[top_rows + 2 * ROWS : top_rows + 3 * ROWS]
            rows16 = lax.broadcasted_iota(jnp.int32, (ROWS, 2 * LANES), 0)
            line = jnp.sum(jnp.where(rows16 == at, sums, 0.0), axis=0, keepdims=True) + add[K : K + 1]
            re, im = line[:, :LANES], line[:, LANES:]
            rls = [b[2] & (LANES - 1) for b in mine]
            cv = chain(which[:1], [pcol_c[pl.ds(rl, 1), :] for rl in rls])
            sv = chain(which[:1], [pcol_s[pl.ds(rl, 1), :] for rl in rls])
            weight = chain(which[:1], [ctf[b[0], 4, :1] for b in mine])
            out_re, out_im = (re * cv - im * sv) * weight, (re * sv + im * cv) * weight
            flats = [jnp.where(sub == q, out_re, jnp.where(sub == groups + q, out_im, flats[0]))]

            for j, (m, top, left) in enumerate(mine):
                total = None
                for g in range(4):
                    shift = (K * (g - j)) % LANES
                    piece = pltpu.roll(values[g], shift, 1) if shift else values[g]
                    total = piece if total is None else jnp.where(which == g, piece, total)
                rt, rl = top & (STEP - 1), left & (LANES - 1)
                cu, su = prow_c[rt], prow_s[rt]
                cv, sv = pcol_c[pl.ds(rl, 1), :], pcol_s[pl.ds(rl, 1), :]
                a = (cu * cv - su * sv) * ctf[m, 0]
                b = (su * cv + cu * sv) * ctf[m, 1]
                tiles.append(total * a + flip(total) * b)
        for i in range(slot_cap // 2):
            outgoing[k, i] = jnp.concatenate([tiles[2 * i], tiles[2 * i + 1]], axis=0).astype(BF16)

        rts = [b[1] & (STEP - 1) for b in boxes]
        ends = [b[2] & (ROWS - 1) for b in boxes]
        cu, su = chain(edge_id, [edge_c[rt] for rt in rts]), chain(edge_id, [edge_s[rt] for rt in rts])
        ce = chain(edge_id, [far_c[pl.ds(e, 1), :] for e in ends])
        se = chain(edge_id, [far_s[pl.ds(e, 1), :] for e in ends])
        weight = chain(edge_id, [ctf[b[0], 2] for b in boxes])
        far = far * (cu * ce - su * se) * weight + flip(far) * (su * ce + cu * se) * weight * sign
        low = jnp.where(sub == 2 * groups, labels[pl.ds(peer, 1), :], flats[0])
        outgoing[k, slot_cap // 2] = jnp.concatenate([far, low], axis=0).astype(BF16)

    def two_peers(i, carry):
        k = 2 * i + 1
        first = jnp.dot(lhs_b[...], right_t[...], preferred_element_type=F32)
        gather(k + 1, lhs_a)
        finish(k, first)
        first = jnp.dot(lhs_a[...], right_t[...], preferred_element_type=F32)
        gather(k + 2, lhs_b)
        finish(k + 1, first)
        block_copy(k).start()
        block_copy(k + 1).start()

        @pl.when(i == peers // 6)
        def _():
            own.wait()
            each(depth, lambda d: to_z(d).wait(), 1)
            each(depth, lambda i: to_y(i).start())

        @pl.when(i == peers // 2 - 2)
        def _():
            each(depth, lambda i: to_y(i).wait())
            each(2 * depth, lambda i: to_c(i).start())

        return carry

    info_copy.wait()
    gather(0, lhs_a)
    first = jnp.dot(lhs_a[...], right_t[...], preferred_element_type=F32)
    gather(1, lhs_b)
    finish(0, first)
    block_copy(0).start()
    lax.fori_loop(0, peers // 2 - 1, two_peers, 0)
    finish(peers - 1, jnp.dot(lhs_b[...], right_t[...], preferred_element_type=F32))
    mine = pltpu.make_async_copy(outgoing.at[peers - 1], arrived.at[me], local_sem.at[1])
    mine.start()

    rot_copy.wait()
    turns, classes = rot.shape
    templates = pick.shape[1]
    named = rot[...].astype(F32)
    named = jnp.concatenate([named, jnp.zeros((turns, LANES - classes), F32)], axis=1)
    high = jnp.floor(named * (1.0 / 256))
    start = lax.broadcasted_iota(jnp.int32, (LANES, templates), 0) * turns
    spot = lax.broadcasted_iota(jnp.int32, (LANES, templates), 1) - start
    chosen = jnp.where((spot >= 0) & (spot < turns), 1.0, 0.0).astype(BF16)
    entry = 256 * jnp.dot(high.astype(BF16), chosen, preferred_element_type=F32) + jnp.dot(
        (named - 256 * high).astype(BF16), chosen, preferred_element_type=F32)
    at = lax.broadcasted_iota(jnp.int32, (turns, templates), 1).astype(F32)
    at = at - jnp.floor((at + 0.5) * (1.0 / turns)) * turns
    own = lax.broadcasted_iota(jnp.int32, (turns, templates), 0).astype(F32) == at
    entry = jnp.sum(jnp.where(own, entry, 0.0), axis=0, keepdims=True)
    entry = entry + jnp.floor((entry + 0.5) * (1.0 / shard.shape[0])) * (padded.shape[0] - shard.shape[0])
    ids = lax.broadcasted_iota(jnp.int32, (ROWS, templates), 0)

    def mark(r, carry):
        rows = pl.ds(pl.multiple_of(r * ROWS, ROWS), ROWS)
        pick[rows, :] = jnp.where((ids + r * ROWS).astype(F32) == entry, 1.0, 0.0).astype(BF16)
        return carry

    lax.fori_loop(0, pick.shape[0] // ROWS, mark, 0)
    pick_copy = pltpu.make_async_copy(pick, pick_out, small_sem.at[6])
    pick_copy.start()

    each(2 * depth, lambda i: to_c(i).wait())
    each(peers - 1, lambda k: block_copy(k).wait())
    mine.wait()
    pick_copy.wait()


def score_kernel(groups, tiles, arrived_h, bank_h, pick_h, cos_h, sin_h, edge_h, flat_h, gather_h, out_h,
                 arrived, bank, cos_t, sin_t, edge_t, flat_t, gather_t, pick, spread, extras, where_v, where, out,
                 *scratch):
    halves, (sem, out_sem) = scratch[:-2], scratch[-2:]
    peers = arrived.shape[0] // tiles
    loads = [
        pltpu.make_async_copy(src, dst, sem.at[i])
        for i, (src, dst) in enumerate(
            [(arrived_h, arrived), (edge_h, edge_t), (flat_h, flat_t), (gather_h, gather_t),
             (cos_h, cos_t), (sin_h, sin_t), (bank_h, bank), (pick_h, pick)])
    ]
    for copy in loads:
        copy.start()

    for copy in loads[:3]:
        copy.wait()
    row = lax.broadcasted_iota(jnp.int32, (ROWS, LANES), 0) // GROUP

    def one(step, total):
        for i in range(8):
            p = step * 8 + i
            x = arrived[p * tiles + tiles - 1].astype(F32)
            rows = pl.ds(pl.multiple_of(p * ROWS, ROWS), ROWS)

            def line(s):
                return jnp.broadcast_to(x[s : s + 1], (ROWS, LANES))

            for s in range(8):
                spread[rows, s * LANES : (s + 1) * LANES] = line(s).astype(BF16) * edge_t[...]
            for part in range(2):
                lines = chain(row, [line(8 + part * groups + q) for q in range(groups)])
                spread[rows, (8 + part) * LANES : (9 + part) * LANES] = lines.astype(BF16) * flat_t[...]
            label = x[8 + 2 * groups : 9 + 2 * groups]
            total = total + jnp.where(label > 0.0, label + (p * ROWS - 1).astype(F32), 0.0)
        return total

    total = lax.fori_loop(0, peers // 8, one, jnp.zeros((1, LANES), F32))
    where_v[...] = jnp.broadcast_to(total, (8, LANES)).astype(jnp.int32)
    where_copy = pltpu.make_async_copy(where_v, where, sem.at[len(loads)])
    where_copy.start()
    loads[3].wait()
    extras[...] = jnp.dot(spread[...], gather_t[...], preferred_element_type=F32)
    where_copy.wait()
    for copy in loads[4:]:
        copy.wait()

    rows = CHUNK * SHIFTS

    def write(chunk):
        part = pl.ds(pl.multiple_of(chunk * rows, rows), rows)
        return pltpu.make_async_copy(out.at[part], out_h.at[part], out_sem.at[chunk])

    def expand(chunk, lhs):
        for n in range(CHUNK):
            slot = where[0, chunk * CHUNK + n]
            p, i = lax.shift_right_logical(slot, 4), slot & (ROWS - 1)
            pair = arrived[p * tiles + lax.shift_right_logical(i, 1)].astype(F32)
            x = jnp.where((i & 1) == 1, pair[8:], pair[:8])
            to = slice(n * SHIFTS, (n + 1) * SHIFTS)
            for k in range(4):
                re = jnp.broadcast_to(x[k : k + 1], (SHIFTS, LANES))
                im = jnp.broadcast_to(x[4 + k : 5 + k], (SHIFTS, LANES))
                c, s = cos_t[k], sin_t[k]
                lhs[to, k * LANES : (k + 1) * LANES] = (re * c - im * s).astype(BF16)
                lhs[to, (4 + k) * LANES : (5 + k) * LANES] = (re * s + im * c).astype(BF16)
            last = jnp.broadcast_to(extras[pl.ds(slot, 1), :], (8, LANES))
            turned = pltpu.roll(last, EXTRA, 1)
            last, turned = jnp.concatenate([last, last], axis=0), jnp.concatenate([turned, turned], axis=0)
            lhs[to, 8 * LANES :] = (last * cos_t[4] + turned * sin_t[4]).astype(BF16)

    def score(lhs):
        return lax.dot_general(lhs[...], bank[...], (((1,), (1,)), ((), ())),
                               preferred_element_type=F32).astype(BF16)

    def emit(chunk, scores):
        picked = jnp.dot(scores, pick[...], preferred_element_type=F32)
        out[pl.ds(pl.multiple_of(chunk * rows, rows), rows)] = picked.astype(BF16)

    def some(step, carry):
        base = step * len(halves)
        waiting = None
        for half, lhs in enumerate(halves):
            expand(base + half, lhs)
            scores = score(lhs)
            if waiting is not None:
                emit(base + half - 1, waiting)
                write(base + half - 1).start()
            waiting = scores
        emit(base + len(halves) - 1, waiting)
        write(base + len(halves) - 1).start()
        return carry

    chunks = out.shape[0] // rows
    lax.fori_loop(0, chunks // len(halves), some, 0)
    for chunk in range(chunks):
        write(chunk).wait()


VMEM = pl.BlockSpec(memory_space=pltpu.VMEM)
HBM = pl.BlockSpec(memory_space=pltpu.HBM)
ANY = pl.BlockSpec(memory_space=pl.ANY)
SMEM = pl.BlockSpec(memory_space=pltpu.SMEM)


def body(micrographs, mic_defocus, defocus, pick_list, template_bank, rot_index):
    peers = lax.axis_size("dom")
    slot_cap = (P_DEV + peers - 1) // peers * 2
    slot_cap = -(-slot_cap // GROUP) * GROUP
    groups = slot_cap // GROUP
    mics, height, width = micrographs.shape
    row_bits, col_bits = bits(height), bits(width)
    columns = pick_list.shape[1]

    left_t, fix_t, right_t = dft_tables()
    tables = [left_t, fix_t, right_t, swap_table()] + phase_tables() + [fold_table()]
    bank_rows = template_bank.shape[0]
    pad_rows = -(-bank_rows // ROWS) * ROWS
    copies = len(tables) + mics * (width // LANES)
    tiles = slot_cap // 2 + 1
    windows = (height - BOX) // STEP + 1
    dma = pltpu.SemaphoreType.DMA
    templates = rot_index.size
    entries = peers * pad_rows
    arrived, bank, pick = pl.pallas_call(
        functools.partial(crop_kernel, peers, slot_cap, (row_bits, col_bits)),
        out_shape=(
            jax.ShapeDtypeStruct((peers, tiles, ROWS, LANES), BF16),
            jax.ShapeDtypeStruct((peers, pad_rows, AREA), BF16),
            jax.ShapeDtypeStruct((entries, templates), BF16),
        ),
        in_specs=[HBM] * (6 + len(tables)),
        out_specs=(ANY, ANY, ANY),
        scratch_shapes=[
            pltpu.VMEM((mics, width // LANES + 1, (height + SWAP) // ROWS, ROWS, LANES), BF16),
            *[pltpu.VMEM(t.shape, t.dtype) for t in tables],
            pltpu.SMEM((peers, LANES), jnp.int32),
            pltpu.VMEM((peers, LANES), jnp.int32),
            pltpu.SMEM(mic_defocus.shape, jnp.int32),
            pltpu.SMEM(defocus.shape, F32),
            pltpu.VMEM((4, columns), jnp.int32),
            pltpu.VMEM(template_bank.shape, BF16),
            pltpu.VMEM((peers, LANES), F32),
            pltpu.VMEM((mics, windows, width // LANES + 1, 2, ROWS, LANES), BF16),
            pltpu.VMEM((mics, width // LANES + 1, ROWS, LANES), BF16),
            pltpu.VMEM((mics, 6, 8, LANES), F32),
            pltpu.VMEM((groups * (3 * ROWS + SWAP), GROUP * BOX), BF16),
            pltpu.VMEM((groups * (3 * ROWS + SWAP), GROUP * BOX), BF16),
            pltpu.VMEM((pad_rows, AREA), BF16),
            pltpu.VMEM((peers, tiles, ROWS, LANES), BF16),
            dma((copies,)), dma((peers,)), dma((peers,)), dma((2,)), dma((peers,)), dma((peers,)), dma((7,)),
            pltpu.VMEM(rot_index.shape[::-1], jnp.int32),
            pltpu.VMEM((entries, templates), BF16),
        ],
        compiler_params=pltpu.CompilerParams(
            collective_id=0, has_side_effects=True, vmem_limit_bytes=56 << 20),
        name="crop",
    )(pick_list, mic_defocus, defocus, template_bank, rot_index.T,
      micrographs.reshape(mics, height // ROWS, ROWS, width), *[jnp.asarray(t) for t in tables])
    bank = bank.reshape(peers * pad_rows, AREA)

    rows = P_DEV * SHIFTS
    consts = shift_phases() + list(spread_tables(slot_cap))
    out = pl.pallas_call(
        functools.partial(score_kernel, groups, tiles),
        out_shape=jax.ShapeDtypeStruct((rows, templates), BF16),
        in_specs=[HBM] * (3 + len(consts)),
        out_specs=HBM,
        scratch_shapes=[
            pltpu.VMEM((peers * tiles, ROWS, LANES), BF16),
            pltpu.VMEM((entries, AREA), BF16),
            *[pltpu.VMEM(c.shape, c.dtype) for c in consts],
            pltpu.VMEM((entries, templates), BF16),
            pltpu.VMEM((peers * ROWS, 10 * LANES), BF16),
            pltpu.VMEM((peers * ROWS, LANES), F32),
            pltpu.VMEM((8, LANES), jnp.int32),
            pltpu.SMEM((8, LANES), jnp.int32),
            pltpu.VMEM((rows, templates), BF16),
            *[pltpu.VMEM((CHUNK * SHIFTS, AREA), BF16)] * HALVES,
            dma((9,)),
            dma((P_DEV // CHUNK,)),
        ],
        compiler_params=pltpu.CompilerParams(vmem_limit_bytes=56 << 20),
        name="score",
    )(arrived.reshape(peers * tiles, ROWS, LANES), bank, pick, *[jnp.asarray(c) for c in consts])
    return out.reshape(P_DEV, SHIFTS, templates)


def solution(mesh):
    return jax.shard_map(
        body,
        mesh=mesh,
        in_specs=(
            P(("groups", "dom"), None, None),
            P(("groups", "dom")),
            P("groups"),
            P(None, ("groups", "dom")),
            P(("groups", "dom"), None),
            P("groups", None),
        ),
        out_specs=P(("groups", "dom"), None, None),
        check_vma=False,
    )
```

```python
import functools
import math

import jax
import jax.numpy as jnp
import ml_dtypes
import numpy as np
from jax import lax
from jax.experimental import pallas as pl
from jax.experimental.pallas import tpu as pltpu
from jax.sharding import PartitionSpec as P

BOX = 256
K = 32
HALF = K // 2
SH = 4
P_DEV = 96
SHIFTS = SH * SH
LANES = 128
ROWS = 16
STEP = 64
SWAP = STEP // 2
PER_BOX = BOX // STEP
GROUP = 4
CHUNK = 16
HALVES = 6
MAIN = K * K // 2
EXTRA = 64
AREA = 2 * (MAIN + EXTRA)

TWO_PI = 2.0 * math.pi
CHI_SCALE = 0.05
CHI_SHIFT = 0.1

MESH = pl.DeviceIdType.MESH
F32 = jnp.float32
BF16 = jnp.bfloat16


def bf(x):
    return np.asarray(x, np.float32).astype(ml_dtypes.bfloat16)


def turn(product):
    return TWO_PI * np.mod(product, BOX) / BOX


def row_order():
    return [4 * s + g - HALF for g in range(4) for s in range(4)]


def dft_tables():
    pixels = np.arange(BOX)
    scale = 1.0 / math.sqrt(BOX)
    order = np.array(row_order()).reshape(4, 4)
    cosine = np.cos(turn(order[..., None] * pixels)) * scale
    sine = -np.sin(turn(order[..., None] * pixels)) * scale
    rows = np.stack([cosine, sine], axis=1).reshape(K, BOX)
    left = np.zeros((2, PER_BOX * K + ROWS, BOX))
    for b in range(PER_BOX):
        cut = BOX - b * STEP
        left[0, b * K : (b + 1) * K, b * STEP :] = rows[:, :cut]
        left[1, b * K : (b + 1) * K, : b * STEP] = rows[:, cut:]
        left[0, PER_BOX * K + b, b * STEP :] = scale
        left[1, PER_BOX * K + b, : b * STEP] = scale
    left = np.concatenate([left[0], left[1, K:]])
    fix = np.zeros((K + ROWS, 2 * SWAP))
    fix[:K, :SWAP] = rows[:, :SWAP]
    fix[:K, SWAP:] = rows[:, -SWAP:]
    fix[K] = scale
    freq = np.arange(K) - HALF
    right = np.zeros((GROUP, BOX, 2, GROUP, K))
    for j in range(GROUP):
        right[j, :, 0, j] = np.cos(turn(freq[:, None] * pixels)).T * scale
        right[j, :, 1, j] = -np.sin(turn(freq[:, None] * pixels)).T * scale
    return bf(left), bf(fix), bf(right.reshape(GROUP * BOX, 2 * GROUP * K))


def swap_table():
    r = np.arange(ROWS)
    low = [(r < t).astype(float) for t in range(ROWS + 1)]
    high = [-(r >= t).astype(float) for t in range(ROWS + 1)]
    return bf(np.broadcast_to(np.array(low + high)[:, :, None], (2 * ROWS + 2, ROWS, LANES)))


def phase_tables():
    sub, lane = np.arange(8)[:, None], np.arange(LANES)[None, :]
    t = np.arange(STEP)[:, None, None]
    t = np.where(t < SWAP, t, t - STEP)
    rows = turn(t * (4 * (sub % 4) + lane // K - HALF))
    edge = turn(t * (4 * (sub % 4) + lane % 4 - HALF))
    cols = turn(np.arange(LANES)[:, None] * (lane % K - HALF))
    far = turn(np.arange(ROWS)[:, None] * HALF + 0 * lane)
    return [f(x).astype(np.float32) for x in (rows, edge, cols, far) for f in (np.cos, np.sin)]


def fold_table():
    table = np.zeros((MAIN, MAIN + LANES))
    for f in range(MAIN):
        u, v = f // K - HALF, f % K - HALF
        if -u < HALF and -v < HALF:
            table[-u * K + HALF - v, f] = 1
    for lane in range(K):
        table[lane, MAIN + lane] = 1
    for lane in range(1, HALF):
        table[(HALF - lane) * K, MAIN + K + lane] = 1
    return bf(table)


def shift_phases():
    moves = np.arange(SH) - SH // 2
    row_move = np.repeat(moves, SH)[:, None]
    col_move = np.tile(moves, SH)[:, None]
    f = np.arange(MAIN)
    u, v = f // K - HALF, f % K - HALF
    lane = np.arange(EXTRA)
    low = lane < K
    u = np.concatenate([u, np.where(low, 0, lane - K - HALF)])
    v = np.concatenate([v, np.where(low, lane - HALF, HALF)])
    phase = turn(row_move * u + col_move * v)
    cosine, sine = np.cos(phase), np.sin(phase)
    main = [x[:, :MAIN].reshape(SHIFTS, MAIN // LANES, LANES).transpose(1, 0, 2) for x in (cosine, sine)]
    last_c = np.concatenate([cosine[:, MAIN:]] * 2, axis=1)
    last_s = np.concatenate([-sine[:, MAIN:], sine[:, MAIN:]], axis=1)
    return [
        np.concatenate([m, x[None]]).astype(np.float32) for m, x in zip(main, (last_c, last_s), strict=True)
    ]


def spread_tables(slot_cap):
    groups = slot_cap // GROUP
    lane = np.arange(LANES)
    edge = np.zeros((ROWS, LANES))
    flat = np.zeros((ROWS, LANES))
    for i in range(slot_cap):
        q, j = i // GROUP, i % GROUP
        edge[i] = (lane // K == j) & (lane % K // 4 == q)
        flat[i] = lane // K == j
    gather = np.zeros((10, LANES, LANES))
    for s in range(8):
        gather[s, lane, EXTRA * (s // 4) + K + 4 * (s % 4) + lane % 4] = 1
    for part in range(2):
        gather[8 + part, lane, EXTRA * part + lane % K] = 1
    assert 8 + 2 * groups < ROWS and groups * 4 <= K
    return bf(edge), bf(flat), bf(gather.reshape(10 * LANES, LANES))


def bits(n):
    return (n - 1).bit_length()


def flip(x):
    return pltpu.roll(x, 4, 0)


def chain(ids, values):
    total = values[0]
    for i, value in enumerate(values[1:], 1):
        total = jnp.where(ids == i, value, total)
    return total


def crop_kernel(peers, slot_cap, shifts, pick_h, mic_def_h, defocus_h, shard_h, rot_h, mic_h, left_h, fix_h, right_h, swap_h,
                prow_ch, prow_sh, edge_ch, edge_sh, pcol_ch, pcol_sh, far_ch, far_sh, fold_h, arrived, bank, pick_out,
                mic, left_t, fix_t, right_t, swap_t, prow_c, prow_s, edge_c, edge_s, pcol_c, pcol_s, far_c, far_s, fold_t,
                info, info_v, mic_def, defocus, pick_v, shard, labels, aligned, flat, ctf, lhs_a, lhs_b, padded, outgoing, load_sem, send_sem, recv_sem, local_sem, bank_send, bank_recv, small_sem, rot, pick):
    groups = slot_cap // GROUP
    depth = peers // 4
    log_step, stack = STEP.bit_length() - 1, 3 * ROWS + SWAP
    mics, blocks, tiles_high = mic.shape[0], mic.shape[1] - 1, mic.shape[2] - SWAP // ROWS
    me = lax.axis_index("dom")
    my_z, my_y, my_c = me // 4, (me // 2) % 2, me % 2
    row_bits, col_bits = shifts

    tables = [
        pltpu.make_async_copy(src, dst, load_sem.at[i])
        for i, (src, dst) in enumerate(
            [(fold_h, fold_t), (left_h, left_t), (fix_h, fix_t), (right_h, right_t), (swap_h, swap_t),
             (prow_ch, prow_c), (prow_sh, prow_s), (edge_ch, edge_c), (edge_sh, edge_s),
             (pcol_ch, pcol_c), (pcol_sh, pcol_s), (far_ch, far_c), (far_sh, far_s)])
    ]

    def load(m, b):
        return pltpu.make_async_copy(
            mic_h.at[m, :, :, pl.ds(b * LANES, LANES)], mic.at[m, b, pl.ds(0, tiles_high)], load_sem.at[len(tables) + m * blocks + b])

    smalls = [
        pltpu.make_async_copy(src, dst, small_sem.at[i])
        for i, (src, dst) in enumerate(
            [(pick_h, pick_v), (mic_def_h, mic_def), (defocus_h, defocus), (shard_h, shard)])
    ]
    for small in smalls:
        small.start()
    tables[0].start()
    tables[1].start()
    for m in range(mics):
        for b in range(blocks):
            load(m, b).start()
    for table in tables[2:]:
        table.start()
    rot_copy = pltpu.make_async_copy(rot_h, rot, small_sem.at[5])
    rot_copy.start()

    barrier = pltpu.get_barrier_semaphore()

    def greet(k, carry):
        pl.semaphore_signal(barrier, inc=1, device_id={"dom": (me + k) % peers}, device_id_type=MESH)
        return carry

    lax.fori_loop(1, peers, greet, 0)

    smalls[0].wait()
    columns = pick_v.shape[1]
    wide = -(-columns // LANES) * LANES
    picks = pick_v[...]
    if wide > columns:
        picks = jnp.concatenate([picks, jnp.full((picks.shape[0], wide - columns), -1, jnp.int32)], axis=1)
    height, width = mic_h.shape[1] * ROWS, mic_h.shape[3]
    spot = (jnp.clip(picks[:1], 0, mics - 1) << row_bits) + jnp.clip(picks[1:2], 0, height - BOX)
    spot = (spot << col_bits) + jnp.clip(picks[2:3], 0, width - BOX)
    target = picks[3:]
    device = target * (-(-(1 << 22) // P_DEV)) >> 22
    label = target - device * P_DEV
    chosen = lax.broadcasted_iota(jnp.int32, (peers, wide), 0) == device
    pick_lane = lax.broadcasted_iota(jnp.int32, (peers, wide), 1)
    rank = chosen.astype(jnp.int32)
    for power in range((wide - 1).bit_length()):
        rank = rank + jnp.where(pick_lane >= 1 << power, pltpu.roll(rank, 1 << power, 1), 0)
    rank = jnp.where(chosen, rank, 0)
    slot_lane = lax.broadcasted_iota(jnp.int32, (peers, LANES), 1)
    spots = jnp.zeros((peers, LANES), jnp.int32)
    for i in range(slot_cap):
        here = jnp.sum(jnp.where(rank == i + 1, spot, 0), axis=1, keepdims=True)
        spots = jnp.where(slot_lane == i, here, spots)
    info_v[...] = spots
    info_copy = pltpu.make_async_copy(info_v, info, small_sem.at[4])
    info_copy.start()
    named = lax.broadcasted_iota(jnp.int32, (LANES, wide), 0) == label
    labels[...] = lax.dot_general(
        rank.astype(F32).astype(BF16), jnp.where(named, 1.0, 0.0).astype(BF16),
        (((1,), (1,)), ((), ())), preferred_element_type=F32)

    smalls[1].wait()
    smalls[2].wait()
    sub = lax.broadcasted_iota(jnp.int32, (8, LANES), 0)
    lane = lax.broadcasted_iota(jnp.int32, (8, LANES), 1)
    sign = jnp.where(sub < 4, -1.0, 1.0).astype(F32)
    lane_u = 4 * (sub % 4) - HALF
    planes = [
        (lane_u + lane // K, lane % K - HALF),
        (lane_u + lane % 4, 0 * lane + HALF),
        (0 * lane, lane % K - HALF),
    ]
    for m in range(mics):
        value = defocus[mic_def[m]]
        for i, (u, v) in enumerate(planes):
            radius = (u * u + v * v).astype(F32)
            weight = -jnp.sin(CHI_SCALE * value * radius + CHI_SHIFT)
            ctf[m, 2 * i] = weight
            ctf[m, 2 * i + 1] = weight * sign

    tables[0].wait()
    smalls[3].wait()
    half = shard.shape[1] // 4
    upper = jnp.concatenate([shard[:, half : 2 * half], shard[:, 3 * half :]], axis=0)
    folded = jnp.dot(upper, fold_t[...], preferred_element_type=F32)
    rows = shard.shape[0]
    re, im = folded[:rows], folded[rows:]
    last_lane = lax.broadcasted_iota(jnp.int32, (rows, EXTRA), 1)
    im_last = jnp.where(last_lane < K, im[:, half : half + EXTRA], -im[:, half : half + EXTRA])
    padded[...] = jnp.zeros_like(padded)
    padded[:rows] = jnp.concatenate(
        [shard[:, :half].astype(F32) + re[:, :half], shard[:, 2 * half : 3 * half].astype(F32) - im[:, :half],
         re[:, half : half + EXTRA], im_last], axis=1).astype(BF16)

    for m in range(mics):
        for b in range(blocks + 1):
            mic[m, b, tiles_high:] = jnp.zeros((SWAP // ROWS, ROWS, LANES), BF16)

    lane_id = lax.broadcasted_iota(jnp.int32, (ROWS, LANES), 1).astype(F32).astype(BF16)
    row_id = lax.broadcasted_iota(jnp.int32, (ROWS, LANES), 0)
    which = lane // K
    edge_id = (lane % K) // 4 * GROUP + lane // K
    pl.semaphore_wait(barrier, peers - 1)

    def to_z(d):
        there = (my_z + d) % depth
        return pltpu.make_async_remote_copy(
            src_ref=padded, dst_ref=bank.at[me], send_sem=bank_send.at[d], recv_sem=bank_recv.at[d],
            device_id={"dom": there * 4 + me % 4}, device_id_type=MESH)

    def to_y(i):
        row = i * 4 + me % 4
        return pltpu.make_async_remote_copy(
            src_ref=bank.at[row], dst_ref=bank.at[row], send_sem=bank_send.at[depth + i],
            recv_sem=bank_recv.at[depth + i],
            device_id={"dom": my_z * 4 + (1 - my_y) * 2 + my_c}, device_id_type=MESH)

    def to_c(i):
        row = i * 2 + my_c
        return pltpu.make_async_remote_copy(
            src_ref=bank.at[row], dst_ref=bank.at[row], send_sem=bank_send.at[2 * depth + i],
            recv_sem=bank_recv.at[2 * depth + i],
            device_id={"dom": my_z * 4 + my_y * 2 + 1 - my_c}, device_id_type=MESH)

    def each(count, act, first=0):
        def step(i, carry):
            act(i)
            return carry

        lax.fori_loop(first, count, step, 0)

    own = pltpu.make_async_copy(padded, bank.at[me], local_sem.at[0])
    own.start()
    each(depth, lambda d: to_z(d).start(), 1)

    tables[1].wait()
    per = BOX // ROWS
    chunks = tiles_high // per

    def align(step):
        m, b = step // (blocks // 2), step % (blocks // 2) * 2
        sums = []

        def pixels(first, count):
            return jnp.concatenate(
                [mic[m, b + h, pl.ds(first, count)].reshape(count * ROWS, LANES) for h in range(2)], axis=1)

        def keep(n, x):
            for t in range(2):
                for h in range(2):
                    aligned[m, n, b + h, t] = x[t * ROWS : (t + 1) * ROWS, h * LANES : (h + 1) * LANES].astype(BF16)

        size = PER_BOX * K + ROWS
        parts = [jnp.dot(left_t[...], pixels(a * per, per), preferred_element_type=F32) for a in range(chunks)]
        for a in range(chunks - 1):
            x, y = parts[a][:size], parts[a + 1][size:]
            keep(a * PER_BOX, x[:K])
            for n in range(1, PER_BOX):
                keep(a * PER_BOX + n, x[n * K : (n + 1) * K] + y[(n - 1) * K : n * K])
            sums.append(x[PER_BOX * K : PER_BOX * K + PER_BOX] + y[(PER_BOX - 1) * K : (PER_BOX - 1) * K + PER_BOX])
        keep((chunks - 1) * PER_BOX, parts[-1][:K])
        sums.append(parts[-1][PER_BOX * K : PER_BOX * K + PER_BOX])
        sums = jnp.concatenate(sums, axis=0).astype(BF16)
        for h in range(2):
            flat[m, b + h] = sums[:, h * LANES : (h + 1) * LANES]

    def two_steps(i, carry):
        for n in range(4):
            load((4 * i + n) // blocks, (4 * i + n) % blocks).wait()
        align(2 * i)
        align(2 * i + 1)
        return carry

    lax.fori_loop(0, mics * blocks // 4, two_steps, 0)
    for table in tables[2:]:
        table.wait()

    def peer_of(k):
        step = k // 4
        flip_z = jnp.where(step < depth // 2, depth // 2 + step, depth - 1 - step)
        return (my_z ^ flip_z) * 4 + (me + 1 + k) % 4

    def block_copy(k):
        return pltpu.make_async_remote_copy(
            src_ref=outgoing.at[k], dst_ref=arrived.at[me], send_sem=send_sem.at[k], recv_sem=recv_sem.at[k],
            device_id={"dom": peer_of(k)}, device_id_type=MESH)

    def unpack(peer, i):
        packed = info[peer, i]
        left = packed & (2**col_bits - 1)
        top = lax.shift_right_logical(packed, col_bits) & (2**row_bits - 1)
        return lax.shift_right_logical(packed, col_bits + row_bits), top, left

    def gather(k, lhs):
        for i in range(slot_cap):
            q, j = i // GROUP, i % GROUP
            m, top, left = unpack(peer_of(k), i)
            block, rl = pl.ds(lax.shift_right_logical(left, 7), 3), left & (LANES - 1)
            window = lax.shift_right_logical(top + SWAP, log_step)
            span = lax.shift_right_logical(top, log_step - 1)
            odd, cut = span & 1, top & (SWAP - 1)
            mask = lane_id >= rl.astype(F32).astype(BF16)

            def put(t, x):
                rows = pl.ds(q * stack + t * ROWS, ROWS)
                lhs[rows, pl.ds(2 * j * LANES, LANES)] = jnp.where(mask, x[0], x[2])
                lhs[rows, pl.ds((2 * j + 1) * LANES, LANES)] = x[1]

            both = aligned[m, window, block]
            put(0, both[:, 0])
            put(1, both[:, 1])
            put(2, flat[m, block])
            for t in range(SWAP // ROWS):
                tile = span * (SWAP // ROWS) + t
                head, tail = mic[m, block, tile], mic[m, block, tile + per]
                coef = swap_t[jnp.clip(cut - t * ROWS, 0, ROWS) + odd * (ROWS + 1)]
                put(3 + t, (tail - head) * coef)

    def finish(k, first):
        peer = peer_of(k)
        boxes = [unpack(peer, i) for i in range(slot_cap)]
        fixes = []
        for q in range(groups):
            part = first[q * stack + 3 * ROWS : (q + 1) * stack]
            odd = chain(which[:1], [lax.shift_right_logical(boxes[q * GROUP + j][1], log_step - 1) & 1 for j in range(GROUP)])
            odd = jnp.concatenate([odd, odd], axis=1) == 1
            fixes.append(jnp.concatenate([jnp.where(odd, 0.0, part), jnp.where(odd, part, 0.0)], axis=0).astype(BF16))
        fixed = jnp.dot(fix_t[...], jnp.concatenate(fixes, axis=1), preferred_element_type=F32)

        far = None
        flats = [jnp.zeros((8, LANES), F32)]
        tiles = []
        for q in range(groups):
            add = fixed[:, q * 2 * LANES : (q + 1) * 2 * LANES]
            top_rows = q * stack
            values, others = [], []
            for g in range(4):
                x = first[top_rows + 8 * g : top_rows + 8 * g + 8] + add[8 * g : 8 * g + 8]
                cos_part, sin_part = x[:, :LANES], flip(x[:, LANES:]) * sign
                values.append(cos_part + sin_part)
                others.append(cos_part - sin_part)
            mine = boxes[q * GROUP : (q + 1) * GROUP]
            edge = None
            for g in range(4):
                piece = pltpu.roll(others[g], g, 1) if g else others[g]
                edge = piece if edge is None else jnp.where(lane % 4 == g, piece, edge)
            edge = pltpu.roll(edge, 4 * q, 1) if q else edge
            far = edge if far is None else jnp.where(edge_id // GROUP == q, edge, far)

            at = chain(which[:1], [lax.shift_right_logical(b[1] + SWAP, log_step) for b in mine])
            at = jnp.concatenate([at, at], axis=1)
            sums = first[top_rows + 2 * ROWS : top_rows + 3 * ROWS]
            rows16 = lax.broadcasted_iota(jnp.int32, (ROWS, 2 * LANES), 0)
            line = jnp.sum(jnp.where(rows16 == at, sums, 0.0), axis=0, keepdims=True) + add[K : K + 1]
            re, im = line[:, :LANES], line[:, LANES:]
            rls = [b[2] & (LANES - 1) for b in mine]
            cv = chain(which[:1], [pcol_c[pl.ds(rl, 1), :] for rl in rls])
            sv = chain(which[:1], [pcol_s[pl.ds(rl, 1), :] for rl in rls])
            weight = chain(which[:1], [ctf[b[0], 4, :1] for b in mine])
            out_re, out_im = (re * cv - im * sv) * weight, (re * sv + im * cv) * weight
            flats = [jnp.where(sub == q, out_re, jnp.where(sub == groups + q, out_im, flats[0]))]

            for j, (m, top, left) in enumerate(mine):
                total = None
                for g in range(4):
                    shift = (K * (g - j)) % LANES
                    piece = pltpu.roll(values[g], shift, 1) if shift else values[g]
                    total = piece if total is None else jnp.where(which == g, piece, total)
                rt, rl = top & (STEP - 1), left & (LANES - 1)
                cu, su = prow_c[rt], prow_s[rt]
                cv, sv = pcol_c[pl.ds(rl, 1), :], pcol_s[pl.ds(rl, 1), :]
                a = (cu * cv - su * sv) * ctf[m, 0]
                b = (su * cv + cu * sv) * ctf[m, 1]
                tiles.append(total * a + flip(total) * b)
        for i in range(slot_cap // 2):
            outgoing[k, i] = jnp.concatenate([tiles[2 * i], tiles[2 * i + 1]], axis=0).astype(BF16)

        rts = [b[1] & (STEP - 1) for b in boxes]
        ends = [b[2] & (ROWS - 1) for b in boxes]
        cu, su = chain(edge_id, [edge_c[rt] for rt in rts]), chain(edge_id, [edge_s[rt] for rt in rts])
        ce = chain(edge_id, [far_c[pl.ds(e, 1), :] for e in ends])
        se = chain(edge_id, [far_s[pl.ds(e, 1), :] for e in ends])
        weight = chain(edge_id, [ctf[b[0], 2] for b in boxes])
        far = far * (cu * ce - su * se) * weight + flip(far) * (su * ce + cu * se) * weight * sign
        low = jnp.where(sub == 2 * groups, labels[pl.ds(peer, 1), :], flats[0])
        outgoing[k, slot_cap // 2] = jnp.concatenate([far, low], axis=0).astype(BF16)

    def two_peers(i, carry):
        k = 2 * i + 1
        first = jnp.dot(lhs_b[...], right_t[...], preferred_element_type=F32)
        gather(k + 1, lhs_a)
        finish(k, first)
        first = jnp.dot(lhs_a[...], right_t[...], preferred_element_type=F32)
        gather(k + 2, lhs_b)
        finish(k + 1, first)
        block_copy(k).start()
        block_copy(k + 1).start()

        @pl.when(i == peers // 6)
        def _():
            own.wait()
            each(depth, lambda d: to_z(d).wait(), 1)
            each(depth, lambda i: to_y(i).start())

        @pl.when(i == peers // 2 - 2)
        def _():
            each(depth, lambda i: to_y(i).wait())
            each(2 * depth, lambda i: to_c(i).start())

        return carry

    info_copy.wait()
    gather(0, lhs_a)
    first = jnp.dot(lhs_a[...], right_t[...], preferred_element_type=F32)
    gather(1, lhs_b)
    finish(0, first)
    block_copy(0).start()
    lax.fori_loop(0, peers // 2 - 1, two_peers, 0)
    finish(peers - 1, jnp.dot(lhs_b[...], right_t[...], preferred_element_type=F32))
    mine = pltpu.make_async_copy(outgoing.at[peers - 1], arrived.at[me], local_sem.at[1])
    mine.start()

    rot_copy.wait()
    turns, classes = rot.shape
    templates = pick.shape[1]
    named = rot[...].astype(F32)
    named = jnp.concatenate([named, jnp.zeros((turns, LANES - classes), F32)], axis=1)
    high = jnp.floor(named * (1.0 / 256))
    start = lax.broadcasted_iota(jnp.int32, (LANES, templates), 0) * turns
    spot = lax.broadcasted_iota(jnp.int32, (LANES, templates), 1) - start
    chosen = jnp.where((spot >= 0) & (spot < turns), 1.0, 0.0).astype(BF16)
    entry = 256 * jnp.dot(high.astype(BF16), chosen, preferred_element_type=F32) + jnp.dot(
        (named - 256 * high).astype(BF16), chosen, preferred_element_type=F32)
    at = lax.broadcasted_iota(jnp.int32, (turns, templates), 1).astype(F32)
    at = at - jnp.floor((at + 0.5) * (1.0 / turns)) * turns
    own = lax.broadcasted_iota(jnp.int32, (turns, templates), 0).astype(F32) == at
    entry = jnp.sum(jnp.where(own, entry, 0.0), axis=0, keepdims=True)
    entry = entry + jnp.floor((entry + 0.5) * (1.0 / shard.shape[0])) * (padded.shape[0] - shard.shape[0])
    ids = lax.broadcasted_iota(jnp.int32, (ROWS, templates), 0)

    def mark(r, carry):
        rows = pl.ds(pl.multiple_of(r * ROWS, ROWS), ROWS)
        pick[rows, :] = jnp.where((ids + r * ROWS).astype(F32) == entry, 1.0, 0.0).astype(BF16)
        return carry

    lax.fori_loop(0, pick.shape[0] // ROWS, mark, 0)
    pick_copy = pltpu.make_async_copy(pick, pick_out, small_sem.at[6])
    pick_copy.start()

    each(2 * depth, lambda i: to_c(i).wait())
    each(peers - 1, lambda k: block_copy(k).wait())
    mine.wait()
    pick_copy.wait()


def score_kernel(groups, tiles, arrived_h, bank_h, pick_h, cos_h, sin_h, edge_h, flat_h, gather_h, out_h,
                 arrived, bank, cos_t, sin_t, edge_t, flat_t, gather_t, pick, spread, extras, where_v, where, out,
                 *scratch):
    halves, (sem, out_sem) = scratch[:-2], scratch[-2:]
    peers = arrived.shape[0] // tiles
    loads = [
        pltpu.make_async_copy(src, dst, sem.at[i])
        for i, (src, dst) in enumerate(
            [(arrived_h, arrived), (edge_h, edge_t), (flat_h, flat_t), (gather_h, gather_t),
             (cos_h, cos_t), (sin_h, sin_t), (bank_h, bank), (pick_h, pick)])
    ]
    for copy in loads:
        copy.start()

    loads[0].wait()
    row = lax.broadcasted_iota(jnp.int32, (ROWS, LANES), 0) // GROUP

    def one(step, carry):
        for i in range(8):
            p = step * 8 + i
            x = arrived[p * tiles + tiles - 1].astype(F32)
            rows = pl.ds(pl.multiple_of(p * ROWS, ROWS), ROWS)

            def line(s):
                return jnp.broadcast_to(x[s : s + 1], (ROWS, LANES))

            for s in range(8):
                spread[rows, s * LANES : (s + 1) * LANES] = line(s).astype(BF16) * edge_t[...]
            for part in range(2):
                lines = chain(row, [line(8 + part * groups + q) for q in range(groups)])
                spread[rows, (8 + part) * LANES : (9 + part) * LANES] = lines.astype(BF16) * flat_t[...]
        return carry

    def find(step, total):
        for i in range(8):
            p = step * 8 + i
            label = arrived[p * tiles + tiles - 1].astype(F32)[8 + 2 * groups : 9 + 2 * groups]
            total = total + jnp.where(label > 0.0, label + (p * ROWS - 1).astype(F32), 0.0)
        return total

    total = lax.fori_loop(0, peers // 8, find, jnp.zeros((1, LANES), F32))
    where_v[...] = jnp.broadcast_to(total, (8, LANES)).astype(jnp.int32)
    where_copy = pltpu.make_async_copy(where_v, where, sem.at[len(loads)])
    where_copy.start()
    loads[1].wait()
    loads[2].wait()
    lax.fori_loop(0, peers // 8, one, 0)
    loads[3].wait()
    extras[...] = jnp.dot(spread[...], gather_t[...], preferred_element_type=F32)
    where_copy.wait()
    for copy in loads[4:]:
        copy.wait()

    rows = CHUNK * SHIFTS

    def write(chunk):
        part = pl.ds(pl.multiple_of(chunk * rows, rows), rows)
        return pltpu.make_async_copy(out.at[part], out_h.at[part], out_sem.at[chunk])

    def expand(chunk, lhs):
        for n in range(CHUNK):
            slot = where[0, chunk * CHUNK + n]
            p, i = lax.shift_right_logical(slot, 4), slot & (ROWS - 1)
            pair = arrived[p * tiles + lax.shift_right_logical(i, 1)].astype(F32)
            x = jnp.where((i & 1) == 1, pair[8:], pair[:8])
            to = slice(n * SHIFTS, (n + 1) * SHIFTS)
            for k in range(4):
                re = jnp.broadcast_to(x[k : k + 1], (SHIFTS, LANES))
                im = jnp.broadcast_to(x[4 + k : 5 + k], (SHIFTS, LANES))
                c, s = cos_t[k], sin_t[k]
                lhs[to, k * LANES : (k + 1) * LANES] = (re * c - im * s).astype(BF16)
                lhs[to, (4 + k) * LANES : (5 + k) * LANES] = (re * s + im * c).astype(BF16)
            last = jnp.broadcast_to(extras[pl.ds(slot, 1), :], (8, LANES))
            turned = pltpu.roll(last, EXTRA, 1)
            last, turned = jnp.concatenate([last, last], axis=0), jnp.concatenate([turned, turned], axis=0)
            lhs[to, 8 * LANES :] = (last * cos_t[4] + turned * sin_t[4]).astype(BF16)

    def score(lhs):
        return lax.dot_general(lhs[...], bank[...], (((1,), (1,)), ((), ())),
                               preferred_element_type=F32).astype(BF16)

    def emit(chunk, scores):
        picked = jnp.dot(scores, pick[...], preferred_element_type=F32)
        out[pl.ds(pl.multiple_of(chunk * rows, rows), rows)] = picked.astype(BF16)

    def some(step, carry):
        base = step * len(halves)
        waiting = None
        for half, lhs in enumerate(halves):
            expand(base + half, lhs)
            scores = score(lhs)
            if waiting is not None:
                emit(base + half - 1, waiting)
                write(base + half - 1).start()
            waiting = scores
        emit(base + len(halves) - 1, waiting)
        write(base + len(halves) - 1).start()
        return carry

    chunks = out.shape[0] // rows
    lax.fori_loop(0, chunks // len(halves), some, 0)
    for chunk in range(chunks):
        write(chunk).wait()


VMEM = pl.BlockSpec(memory_space=pltpu.VMEM)
HBM = pl.BlockSpec(memory_space=pltpu.HBM)
ANY = pl.BlockSpec(memory_space=pl.ANY)
SMEM = pl.BlockSpec(memory_space=pltpu.SMEM)


def body(micrographs, mic_defocus, defocus, pick_list, template_bank, rot_index):
    peers = lax.axis_size("dom")
    slot_cap = (P_DEV + peers - 1) // peers * 2
    slot_cap = -(-slot_cap // GROUP) * GROUP
    groups = slot_cap // GROUP
    mics, height, width = micrographs.shape
    row_bits, col_bits = bits(height), bits(width)
    columns = pick_list.shape[1]

    left_t, fix_t, right_t = dft_tables()
    tables = [left_t, fix_t, right_t, swap_table()] + phase_tables() + [fold_table()]
    bank_rows = template_bank.shape[0]
    pad_rows = -(-bank_rows // ROWS) * ROWS
    copies = len(tables) + mics * (width // LANES)
    tiles = slot_cap // 2 + 1
    windows = (height - BOX) // STEP + 1
    dma = pltpu.SemaphoreType.DMA
    templates = rot_index.size
    entries = peers * pad_rows
    arrived, bank, pick = pl.pallas_call(
        functools.partial(crop_kernel, peers, slot_cap, (row_bits, col_bits)),
        out_shape=(
            jax.ShapeDtypeStruct((peers, tiles, ROWS, LANES), BF16),
            jax.ShapeDtypeStruct((peers, pad_rows, AREA), BF16),
            jax.ShapeDtypeStruct((entries, templates), BF16),
        ),
        in_specs=[HBM] * (6 + len(tables)),
        out_specs=(ANY, ANY, ANY),
        scratch_shapes=[
            pltpu.VMEM((mics, width // LANES + 1, (height + SWAP) // ROWS, ROWS, LANES), BF16),
            *[pltpu.VMEM(t.shape, t.dtype) for t in tables],
            pltpu.SMEM((peers, LANES), jnp.int32),
            pltpu.VMEM((peers, LANES), jnp.int32),
            pltpu.SMEM(mic_defocus.shape, jnp.int32),
            pltpu.SMEM(defocus.shape, F32),
            pltpu.VMEM((4, columns), jnp.int32),
            pltpu.VMEM(template_bank.shape, BF16),
            pltpu.VMEM((peers, LANES), F32),
            pltpu.VMEM((mics, windows, width // LANES + 1, 2, ROWS, LANES), BF16),
            pltpu.VMEM((mics, width // LANES + 1, ROWS, LANES), BF16),
            pltpu.VMEM((mics, 6, 8, LANES), F32),
            pltpu.VMEM((groups * (3 * ROWS + SWAP), GROUP * BOX), BF16),
            pltpu.VMEM((groups * (3 * ROWS + SWAP), GROUP * BOX), BF16),
            pltpu.VMEM((pad_rows, AREA), BF16),
            pltpu.VMEM((peers, tiles, ROWS, LANES), BF16),
            dma((copies,)), dma((peers,)), dma((peers,)), dma((2,)), dma((peers,)), dma((peers,)), dma((7,)),
            pltpu.VMEM(rot_index.shape[::-1], jnp.int32),
            pltpu.VMEM((entries, templates), BF16),
        ],
        compiler_params=pltpu.CompilerParams(
            collective_id=0, has_side_effects=True, vmem_limit_bytes=56 << 20),
        name="crop",
    )(pick_list, mic_defocus, defocus, template_bank, rot_index.T,
      micrographs.reshape(mics, height // ROWS, ROWS, width), *[jnp.asarray(t) for t in tables])
    bank = bank.reshape(peers * pad_rows, AREA)

    rows = P_DEV * SHIFTS
    consts = shift_phases() + list(spread_tables(slot_cap))
    out = pl.pallas_call(
        functools.partial(score_kernel, groups, tiles),
        out_shape=jax.ShapeDtypeStruct((rows, templates), BF16),
        in_specs=[HBM] * (3 + len(consts)),
        out_specs=HBM,
        scratch_shapes=[
            pltpu.VMEM((peers * tiles, ROWS, LANES), BF16),
            pltpu.VMEM((entries, AREA), BF16),
            *[pltpu.VMEM(c.shape, c.dtype) for c in consts],
            pltpu.VMEM((entries, templates), BF16),
            pltpu.VMEM((peers * ROWS, 10 * LANES), BF16),
            pltpu.VMEM((peers * ROWS, LANES), F32),
            pltpu.VMEM((8, LANES), jnp.int32),
            pltpu.SMEM((8, LANES), jnp.int32),
            pltpu.VMEM((rows, templates), BF16),
            *[pltpu.VMEM((CHUNK * SHIFTS, AREA), BF16)] * HALVES,
            dma((9,)),
            dma((P_DEV // CHUNK,)),
        ],
        compiler_params=pltpu.CompilerParams(vmem_limit_bytes=56 << 20),
        name="score",
    )(arrived.reshape(peers * tiles, ROWS, LANES), bank, pick, *[jnp.asarray(c) for c in consts])
    return out.reshape(P_DEV, SHIFTS, templates)


def solution(mesh):
    return jax.shard_map(
        body,
        mesh=mesh,
        in_specs=(
            P(("groups", "dom"), None, None),
            P(("groups", "dom")),
            P("groups"),
            P(None, ("groups", "dom")),
            P(("groups", "dom"), None),
            P("groups", None),
        ),
        out_specs=P(("groups", "dom"), None, None),
        check_vma=False,
    )
```
